128 devices in a mesh: ctx: 16 (over y, z), seq: 8 (over x, core).
Axes of the slice: x: 4, y: 4, z: 4, core: 2. Of those that a mesh axis runs over, the one named last changes fastest.
Arguments:
- query_matrix: bfloat16 [131072, 2048], P(('seq', 'ctx')), parts along dimension 0, may hold values from -7 to 7
- key_vectors: bfloat16 [131072, 2048], P(('seq', 'ctx')), parts along dimension 0, may hold values from -7.5 to 7.5
- value_vectors: bfloat16 [131072, 4096], P(('seq', 'ctx')), parts along dimension 0, may hold values from -6 to 6
- input_gate: float32 [8, 131072], P(None, ('seq', 'ctx')), parts along dimension 1, may hold values from -4 to 300
- forget_gate: float32 [8, 131072], P(None, ('seq', 'ctx')), parts along dimension 1, may hold values from 0 to 12.7
Outputs:
- hidden_state: bfloat16 [131072, 4096], P(('seq', 'ctx')), parts along dimension 0
- final_memory: float32 [64, 256, 512], P('seq', 'ctx'), parts along dimension 0
- final_normalizer: float32 [64, 256], P('seq', 'ctx'), parts along dimension 0
- final_stabilizer: float32 [64], P('seq'), parts along dimension 0
The draws below stay inside these ranges and needn't reach their ends.
There are 8 independent parts, one for each index of `seq`. The reference program is written for one: setup_inputs(seed, part) draws one part's arguments, and reference() takes and returns one part's arrays. A program takes and returns all parts, laid end to end along the dimension named above; each array names one. Nothing has to cross between parts.
All inputs are finite; a program needn't handle non-finite values.
Results may differ from the reference program's by a relative error of at most 0.0056.
Values sent between devices are 32-bit elements; how exact they have to be, the bound alone decides.
A program may use at most 192 MiB of HBM per device.

```python
import math
import jax
import jax.numpy as jnp
from jax import lax

H = 8
DQK = 256
DV = 512
TOK_DEV = 1024
TOKENS = 16384
N_CTX = 16


def draw_query_matrix(key, part):
    base = jnp.clip(jax.random.normal(jax.random.fold_in(key, 21), (TOKENS, H * DQK), jnp.float32), -6.0, 6.0)
    return base.astype(jnp.bfloat16)


def draw_key_vectors(key, part):
    base = jnp.clip(jax.random.normal(jax.random.fold_in(key, 22), (TOKENS, H * DQK), jnp.float32), -6.0, 6.0)
    return base.astype(jnp.bfloat16)


def draw_forget_gate(key, part):
    subkeys = jax.random.split(key, 6)
    order = jax.random.permutation(subkeys[0], H)
    slow = order < H // 2
    base = jnp.where(slow, jax.random.uniform(subkeys[1], (H,), jnp.float32, 10.0, 12.0), jax.random.uniform(subkeys[2], (H,), jnp.float32, 2.5, 4.5))
    coarse_estimate = base[:, None] + jax.random.uniform(subkeys[3], (H, TOKENS), jnp.float32, -0.7, 0.7)
    spots = jax.random.randint(subkeys[4], (3,), 0, TOKENS)
    gate_magnitudes = jax.random.uniform(subkeys[5], (3,), jnp.float32, 0.0, 1.4)
    places = jnp.arange(TOKENS)
    spike_positions = places[None, :] == spots[:, None]
    sudden_surge = jnp.max(jnp.where(spike_positions, gate_magnitudes[:, None], -1.0), axis=0)
    return jnp.where(sudden_surge[None, :] >= 0.0, sudden_surge[None, :], coarse_estimate).astype(jnp.float32)


def draw_input_gate(key, part):
    subkeys = jax.random.split(key, 1)
    base = jax.random.uniform(subkeys[0], (H, TOKENS), jnp.float32, -4.0, 2.0)
    return base.astype(jnp.float32)


def steps_of(stream_key, shape, shards, least, high):
    def one(dim, parts):
        steps = jax.random.uniform(jax.random.fold_in(jax.random.fold_in(stream_key, 6), dim), (parts,), jnp.float32, least / len(shards), high / len(shards))
        return jnp.repeat(jnp.exp(steps), shape[dim] // parts).reshape((-1,) + (1,) * (len(shape) - dim - 1))

    loudness = one(*shards[0])
    for cut in shards[1:]:
        loudness = loudness * one(*cut)
    return loudness


def noise(rng, dims, spread, most, pieces=(), held_as=jnp.bfloat16):
    values = spread * jax.random.normal(rng, dims, jnp.float32)
    if pieces:
        values = values * steps_of(rng, dims, pieces, -0.22, 0.18)
    return jnp.clip(values, -most, most).astype(held_as)


def setup_inputs(seed: int = 0, part: int = 0) -> dict:
    splits = jax.random.split(jax.random.key(seed), 6)
    part_keys = jax.random.split(jax.random.fold_in(splits[5], part), 6)
    return {
        "query_matrix": draw_query_matrix(jax.random.fold_in(jax.random.fold_in(splits[5], part), 71), part),
        "key_vectors": draw_key_vectors(jax.random.fold_in(jax.random.fold_in(splits[5], part), 71), part),
        "value_vectors": noise(part_keys[2], (TOKENS, H * DV), 1.0, 6.0, ((0, 16),)),
        "input_gate": draw_input_gate(jax.random.fold_in(jax.random.fold_in(splits[5], part), 71), part),
        "forget_gate": draw_forget_gate(jax.random.fold_in(jax.random.fold_in(splits[5], part), 71), part),
    }


VERY_NEGATIVE = -1e+30

def summarize(key_vectors, value_vectors, input_gate, cumulated):
    decay_sum = cumulated[:, -1]
    exponent = decay_sum[:, None] - cumulated + input_gate
    stabilizer = lax.optimization_barrier(jnp.max(exponent, axis=1))
    weight = jnp.exp(exponent - stabilizer[:, None])

    def one_head(head_index):
        key_rows = lax.dynamic_slice_in_dim(key_vectors, head_index * DQK, DQK, 1).astype(jnp.float32)
        value_rows = lax.dynamic_slice_in_dim(value_vectors, head_index * DV, DV, 1)
        scaled = key_rows * weight[head_index][:, None]
        matrix_memory = lax.dot_general(scaled.astype(jnp.bfloat16), value_rows, (((0,), (0,)), ((), ())), preferred_element_type=jnp.float32)
        return (matrix_memory, lax.optimization_barrier(jnp.sum(scaled, axis=0)))
    matrix_memory, normal = lax.map(one_head, jnp.arange(H, dtype=jnp.int32))
    return (matrix_memory, normal, stabilizer, decay_sum)

def combine(earlier, later):
    first_memory, first_normal, first_stab, first_decay = earlier
    second_memory, second_normal, second_stab, second_decay = later
    stabilizer = jnp.maximum(first_stab + second_decay, second_stab)
    first_scale = jnp.exp(first_stab + second_decay - stabilizer)
    second_scale = jnp.exp(second_stab - stabilizer)
    matrix_memory = first_memory * first_scale[..., None, None] + second_memory * second_scale[..., None, None]
    normal = first_normal * first_scale[..., None] + second_normal * second_scale[..., None]
    return (matrix_memory, normal, stabilizer, first_decay + second_decay)

def block_output(query_matrix, key_vectors, value_vectors, input_gate, cumulated, prefix_memory, prefix_normal, prefix_stab):
    length = query_matrix.shape[0]
    scaling = 1.0 / math.sqrt(DQK)
    memory_b = prefix_memory.astype(jnp.bfloat16)
    row_index = lax.broadcasted_iota(jnp.int32, (length, length), 0)
    col_index = lax.broadcasted_iota(jnp.int32, (length, length), 1)
    causal = row_index >= col_index

    def one_head(head_index, out_buffer):
        head_index = jnp.asarray(head_index).astype(jnp.int32)
        query_rows = lax.dynamic_slice_in_dim(query_matrix, head_index * DQK, DQK, 1)
        key_rows = lax.dynamic_slice_in_dim(key_vectors, head_index * DQK, DQK, 1)
        value_rows = lax.dynamic_slice_in_dim(value_vectors, head_index * DV, DV, 1)
        scores = lax.dot_general(query_rows, key_rows, (((1,), (1,)), ((), ())), preferred_element_type=jnp.float32) * scaling
        cum_head = cumulated[head_index]
        gate_head = input_gate[head_index]
        exponent = jnp.where(causal, cum_head[:, None] - cum_head[None, :] + gate_head[None, :], VERY_NEGATIVE)
        carried = cum_head + prefix_stab[head_index]
        stabilizer = jnp.maximum(carried, lax.optimization_barrier(jnp.max(exponent, axis=1)))
        weights = jnp.where(causal, jnp.exp(exponent - stabilizer[:, None]) * scores, 0.0)
        factor = jnp.exp(carried - stabilizer)
        carried_term = jnp.dot(query_rows, memory_b[head_index], preferred_element_type=jnp.float32) * scaling
        numerator = factor[:, None] * carried_term + jnp.dot(weights.astype(jnp.bfloat16), value_rows, preferred_element_type=jnp.float32)
        query_normal = lax.optimization_barrier(jnp.sum(query_rows.astype(jnp.float32) * prefix_normal[head_index][None, :], axis=1)) * scaling
        denominator = factor * query_normal + lax.optimization_barrier(jnp.sum(weights, axis=1))
        result = numerator / jnp.maximum(jnp.abs(denominator), jnp.exp(-stabilizer))[:, None]
        return lax.dynamic_update_slice_in_dim(out_buffer, result.astype(jnp.bfloat16), head_index * DV, 1)
    return lax.fori_loop(0, H, one_head, jnp.zeros((length, H * DV), jnp.bfloat16))

def reference(query_matrix, key_vectors, value_vectors, input_gate, forget_gate):
    log_forget = jax.nn.log_sigmoid(forget_gate)
    cumulated = jnp.cumsum(log_forget.reshape(H, N_CTX, TOK_DEV).transpose(1, 0, 2), axis=2)
    gate_blocks = input_gate.reshape(H, N_CTX, TOK_DEV).transpose(1, 0, 2)
    query_segments = query_matrix.reshape(N_CTX, TOK_DEV, H * DQK)
    key_blocks = key_vectors.reshape(N_CTX, TOK_DEV, H * DQK)
    value_blocks = value_vectors.reshape(N_CTX, TOK_DEV, H * DV)
    identity = (jnp.zeros((H, DQK, DV), jnp.float32), jnp.zeros((H, DQK), jnp.float32), jnp.full((H,), VERY_NEGATIVE, jnp.float32), jnp.zeros((H,), jnp.float32))

    def advance(prefix, block_data):
        queries_here, keys_here, values_here, gates_here, cum_here = block_data
        output = block_output(queries_here, keys_here, values_here, gates_here, cum_here, prefix[0], prefix[1], prefix[2])
        own_summary = summarize(keys_here, values_here, gates_here, cum_here)
        return (combine(prefix, own_summary), output)
    final_state, outputs = lax.scan(advance, identity, (query_segments, key_blocks, value_blocks, gate_blocks, cumulated))
    return (outputs.reshape(TOKENS, H * DV), final_state[0], final_state[1], final_state[2])
```

```python
import functools

import jax
import jax.numpy as jnp
from jax import lax
from jax.experimental import pallas as pl
from jax.experimental.pallas import tpu as pltpu
from jax.sharding import Mesh
from jax.sharding import PartitionSpec as P

H = 8
DQK = 256
DV = 512
LEN = 1024
NY = 4
NZ = 4
CTX = ("ctx_0", "ctx_1")
SEQ_CTX = ("seq", "ctx_0", "ctx_1")
NEG = -1e30
F32 = jnp.float32
BF16 = jnp.bfloat16
MESH = pl.DeviceIdType.MESH

PATHS = {
    1: (2, 1, 0, 3),
    2: (2, 3, 0, 1),
    3: (3, 2, 1, 0),
    4: (0, 1, 2, 3),
    5: (1, 2, 3, 0),
    6: (1, 0, 3, 2),
}
KINDS = (1, 5, 3, 6, 4, 2, 1, 5)
ZC = {1: (1, 1, 0), 2: (0, 1, 0), 3: (0, 0, 0), 4: (1, 1, 0), 5: (0, 0, 0), 6: (1, 0, 0)}
ZB = {1: (0, 1, 0), 2: (0, 1, 1), 3: (0, 1, 1), 4: (0, 0, 0), 5: (0, 0, 1), 6: (0, 0, 0)}
PO = {1: (0, 0, 0), 2: (0, 0, 0), 3: (0, 0, 1), 4: (1, 0, 0), 5: (1, 0, 1), 6: (1, 0, 1)}
PB_A = {1: 0, 2: 1, 3: 0, 4: 1, 5: 1, 6: 0}
ZA_B = {1: 1, 2: 0, 3: 1, 4: 0, 5: 0, 6: 1}

PIECES = 4
ROWS = DQK // PIECES
UNITS = H * PIECES
LAG_O = 2
LAG_Y = 2
LAG_B = 2
LAG_E = 2
NCOEF = 22
TILE = 256


def pick(h, values):
    out = jnp.int32(values[-1])
    for i in range(len(values) - 1):
        out = jnp.where(h == i, jnp.int32(values[i]), out)
    return out


def kernel(
    q_hbm, k_hbm, v_hbm, gate_ref, forget_ref,
    out_hbm, finm_ref, fins_ref,
    qs, ks, vs, mem, land1, land2, land3, send1, acc, pref,
    cols1, cols2, dens, rows_tmp, arow, rowst, ctab, stats, norms, pnorm, fin,
    in_sem, out_sem, r1, r2, r3, s0, s1, s2, sf, rf, rstat, rnorm, sstat, snorm, loc_sem,
):
    y = lax.axis_index("ctx_0")
    z = lax.axis_index("ctx_1")
    me = y * NZ + z

    def remote(src, dst, ss, rs, yy, zz):
        return pltpu.make_async_remote_copy(
            src_ref=src, dst_ref=dst, send_sem=ss, recv_sem=rs,
            device_id={"ctx_0": yy, "ctx_1": zz}, device_id_type=MESH,
        )

    def load(hbm, dst, h, width, sem):
        return pltpu.make_async_copy(hbm.at[:, h * width:(h + 1) * width], dst.at[h], sem)

    loads = []
    for h in range(H):
        loads.append((
            load(k_hbm, ks, h, DQK, in_sem.at[h]),
            load(v_hbm, vs, h, DV, in_sem.at[H + h]),
            load(q_hbm, qs, h, DQK, in_sem.at[2 * H + h]),
        ))
    for h in range(H):
        loads[h][0].start()
        loads[h][1].start()
    for h in range(H):
        loads[h][2].start()

    barrier = pltpu.get_barrier_semaphore()

    def greet(i, _):
        peer = lax.rem(me + i, NY * NZ)
        pl.semaphore_signal(
            barrier, inc=1,
            device_id={"ctx_0": peer // NZ, "ctx_1": lax.rem(peer, NZ)}, device_id_type=MESH,
        )
        return 0

    lax.fori_loop(1, NY * NZ, greet, 0)

    lane = lax.broadcasted_iota(jnp.int32, (H, LEN), 1)
    f = forget_ref[...]
    cum = jnp.minimum(f, 0.0) - jnp.log1p(jnp.exp(-jnp.abs(f)))
    for s in (1, 2, 4, 8, 16, 32, 64, 128, 256, 512):
        cum = cum + jnp.where(lane >= s, pltpu.roll(cum, s, 1), 0.0)
    a = gate_ref[...] - cum
    b0 = a
    for s in (1, 2, 4, 8, 16, 32, 64, 128, 256, 512):
        b0 = jnp.maximum(b0, jnp.where(lane >= s, pltpu.roll(b0, s, 1), NEG))
    arow[...] = a
    rowst[0] = b0
    rowst[1] = cum
    amax = b0[:, LEN - 1:LEN]
    rows_tmp[...] = jnp.zeros_like(rows_tmp)
    rows_tmp[0:H, :] = jnp.exp(a - amax)
    rows_tmp[H:2 * H, :] = b0
    cols1[...] = rows_tmp[...].T
    decay = cum[:, LEN - 1:LEN]
    stats[me, 0:H] = jnp.broadcast_to(decay + amax, (H, 128))
    stats[me, H:2 * H] = jnp.broadcast_to(decay, (H, 128))
    dens[...] = jnp.zeros_like(dens)

    pl.semaphore_wait(barrier, NY * NZ - 1)

    def spread(table, ss, rs):
        def one(i, _):
            peer = lax.rem(me + i, NY * NZ)
            remote(table.at[me], table.at[me], ss.at[peer], rs.at[me], peer // NZ, lax.rem(peer, NZ)).start()
            return 0
        lax.fori_loop(1, NY * NZ, one, 0)

    def gathered(table, ss, rs):
        def one(i, _):
            peer = lax.rem(me + i, NY * NZ)
            remote(table.at[peer], table.at[peer], ss.at[peer], rs.at[peer], y, z).wait_recv()
            return 0
        lax.fori_loop(1, NY * NZ, one, 0)

    def spread_done(table, ss, rs):
        def one(i, _):
            peer = lax.rem(me + i, NY * NZ)
            remote(table.at[me], table.at[me], ss.at[peer], rs.at[me], y, z).wait_send()
            return 0
        lax.fori_loop(1, NY * NZ, one, 0)

    spread(stats, sstat, rstat)

    def path(h):
        return tuple(pick(h, [PATHS[k][i] for k in KINDS]) for i in range(4))

    def unit(u):
        h = u // PIECES
        c = u - h * PIECES
        return h, c, pl.ds(pl.multiple_of(c * ROWS, ROWS), ROWS)

    def column(table, start, size, h, base):
        x = pltpu.roll(table[pl.ds(start, size), :], lax.rem(128 - h, 128), 1)
        return x[:, base:base + 1]

    def summarize(h, _):
        pltpu.make_async_copy(k_hbm.at[:, 0:DQK], ks.at[h], in_sem.at[h]).wait()
        pltpu.make_async_copy(v_hbm.at[:, 0:DV], vs.at[h], in_sem.at[H + h]).wait()
        scaled = ks[h].astype(F32) * column(cols1, 0, LEN, h, 0)
        norms[me, pl.ds(h, 1), :] = jnp.sum(scaled, axis=0, keepdims=True)
        mem[h] = lax.dot_general(
            scaled.astype(BF16), vs[h], (((0,), (0,)), ((), ())), preferred_element_type=F32
        )
        na, nb, no, nc = path(h)
        for c in range(PIECES):
            u = h * PIECES + c
            rows = pl.ds(c * ROWS, ROWS)

            @pl.when(z == na)
            def _():
                remote(mem.at[h, rows], land1.at[h, rows], s0.at[u], r1.at[u], y, nb).start()

            @pl.when(z == nc)
            def _():
                remote(mem.at[h, rows], land2.at[h, rows], s0.at[u], r2.at[u], y, no).start()
        return 0

    lax.fori_loop(0, H, summarize, 0)
    spread(norms, snorm, rnorm)

    gathered(stats, sstat, rstat)
    sub = lax.broadcasted_iota(jnp.int32, (H, 128), 0)

    def by_head(table):
        out = jnp.zeros((H, 128), F32)
        for h in range(H):
            if table[KINDS[h]] != 0:
                out = jnp.where(sub == h, 1.0, out)
        return out > 0.5

    total = jnp.zeros((H, 128), F32)
    before = jnp.zeros((H, 128), F32)
    top_row = jnp.full((H, 128), NEG, F32)
    top_me = jnp.full((H, 128), NEG, F32)
    top_all = jnp.full((H, 128), NEG, F32)
    logs = []
    for i in range(NY * NZ):
        before = jnp.where(me == i, total, before)
        dec = stats[i, H:2 * H]
        total = total + dec
        w = stats[i, 0:H] - total
        logs.append(w)
        top_row = jnp.maximum(top_row, jnp.where(i < y * NZ, w, NEG))
        top_me = jnp.maximum(top_me, jnp.where(i < me, w, NEG))
        top_all = jnp.maximum(top_all, w)
    here = []
    for j in range(NZ):
        w = logs[j]
        for r in range(1, NY):
            w = jnp.where(y == r, logs[r * NZ + j], w)
        here.append(w)

    def node(i):
        out = here[0]
        for j in range(1, NZ):
            mask = by_head({k: int(PATHS[k][i] == j) for k in PATHS})
            out = jnp.where(mask, here[j], out)
        return out

    l_a, l_b, l_o, l_c = (node(i) for i in range(4))
    l_ab = jnp.maximum(l_a, l_b)
    coefs = [jnp.exp(l_a - l_ab), jnp.exp(l_b - l_ab)]

    def union(base, parts):
        top = base
        for value, mask in parts:
            top = jnp.maximum(top, value if mask is None else jnp.where(mask, value, NEG))
        out = [jnp.exp(base - top)]
        for value, mask in parts:
            e = jnp.exp(value - top)
            out.append(e if mask is None else jnp.where(mask, e, 0.0))
        return top, out

    coefs += union(top_row, [(l_ab, None), (l_o, None), (l_c, None)])[1]
    tops = {}
    for name, table in (("c", ZC), ("b", ZB), ("o", PO)):
        masks = [by_head({k: table[k][i] for k in table}) for i in range(3)]
        tops[name], cs = union(top_row, list(zip((l_ab, l_o, l_c), masks)))
        coefs += cs
    coefs += union(tops["b"], [(l_a, by_head(PB_A))])[1]
    coefs += union(tops["b"], [(l_b, by_head(ZA_B))])[1]
    for i, cf in enumerate(coefs):
        ctab[i] = jnp.concatenate([cf] * (DV // 128), axis=1)

    carried = top_me + before
    prefix_top = carried[:, 0:1]
    b0 = rowst[0]
    cum = rowst[1]
    b = jnp.maximum(prefix_top, b0)
    rows_tmp[0:H, :] = jnp.exp(prefix_top - b) * (1.0 / 16.0)
    rows_tmp[H:2 * H, :] = jnp.exp(b0 - b) * (1.0 / 16.0)
    rows_tmp[2 * H:3 * H, :] = jnp.exp(-(cum + b))
    cols2[...] = rows_tmp[...].T
    fins_ref[H:2 * H, :] = top_all + total

    def normals():
        gathered(norms, snorm, rnorm)
        tot = jnp.zeros((H, DQK), F32)
        mine = jnp.zeros((H, DQK), F32)
        for i in range(NY * NZ):
            n = norms[i]
            w_all = jnp.exp(logs_ref(i) - top_all[:, 0:1])
            w_me = jnp.where(i < me, jnp.exp(logs_ref(i) - top_me[:, 0:1]), 0.0)
            tot = tot + w_all * n
            mine = mine + w_me * n
        pnorm[0:H, :] = mine
        turned = pltpu.roll(tot, lax.rem(DQK - me * (DQK // (NY * NZ)), DQK), 1)
        fins_ref[0:H, :] = turned[:, 0:128]

    def logs_ref(i):
        return logs[i][:, 0:1]

    def coef(i, h):
        return ctab[i, pl.ds(h, 1), :]

    STEP = 16

    def gather_b(u):
        h, c, rows = unit(u)
        na, nb, no, nc = path(h)

        @pl.when(z == nb)
        def _():
            remote(mem.at[h, rows], land1.at[h, rows], s0.at[u], r1.at[u], y, no).wait_recv()
            for t in range(ROWS // STEP):
                part = pl.ds(pl.multiple_of(c * ROWS + t * STEP, STEP), STEP)
                send1[h, part] = coef(0, h) * land1[h, part] + coef(1, h) * mem[h, part]
            remote(send1.at[h, rows], land1.at[h, rows], s0.at[u], r1.at[u], y, no).start()

    def own_o(u):
        h, c, rows = unit(u)
        na, nb, no, nc = path(h)

        @pl.when(z == no)
        def _():
            remote(mem.at[h, rows], land1.at[h, rows], s0.at[u], r1.at[u], y, nb).wait_recv()
            remote(mem.at[h, rows], land2.at[h, rows], s0.at[u], r2.at[u], y, nb).wait_recv()

            @pl.when(y == 0)
            def _():
                land3[h, rows] = jnp.zeros((ROWS, DV), F32)

            @pl.when(y > 0)
            def _():
                remote(mem.at[h, rows], land3.at[h, rows], s0.at[u], r3.at[u], y, nb).wait_recv()

            for t in range(ROWS // STEP):
                part = pl.ds(pl.multiple_of(c * ROWS + t * STEP, STEP), STEP)
                r = land3[h, part]
                xb = land1[h, part]
                xc = land2[h, part]
                mo = mem[h, part]

                def mix(i):
                    return coef(i, h) * r + coef(i + 1, h) * xb + coef(i + 2, h) * mo + coef(i + 3, h) * xc

                send1[h, part] = mix(2)
                land2[h, part] = mix(6)
                land1[h, part] = mix(10)
                pref[h, part] = mix(14).astype(BF16)

            @pl.when(y < NY - 1)
            def _():
                remote(send1.at[h, rows], land3.at[h, rows], s0.at[u], r3.at[u], y + 1, z).start()

            remote(land1.at[h, rows], land3.at[h, rows], s1.at[u], r3.at[u], y, nb).start()
            remote(land2.at[h, rows], land3.at[h, rows], s2.at[u], r3.at[u], y, nc).start()

            @pl.when(y == NY - 1)
            def _():
                for j in range(NZ):
                    part = pl.ds(pl.multiple_of(c * ROWS + j * STEP, STEP), STEP)

                    @pl.when((c != NY - 1) | (z != j))
                    def _():
                        remote(send1.at[h, part], fin.at[h], sf.at[u * NZ + j], rf.at[h], c, j).start()

                    @pl.when((c == NY - 1) & (z == j))
                    def _():
                        fin[h] = send1[h, part]

    def back_b(u):
        h, c, rows = unit(u)
        na, nb, no, nc = path(h)

        @pl.when(z == nb)
        def _():
            remote(mem.at[h, rows], land3.at[h, rows], s0.at[u], r3.at[u], y, no).wait_recv()
            for t in range(ROWS // STEP):
                part = pl.ds(pl.multiple_of(c * ROWS + t * STEP, STEP), STEP)
                zb = land3[h, part]
                pref[h, part] = (coef(18, h) * zb + coef(19, h) * land1[h, part]).astype(BF16)
                land3[h, part] = coef(20, h) * zb + coef(21, h) * mem[h, part]
            remote(land3.at[h, rows], land3.at[h, rows], s1.at[u], r3.at[u], y, na).start()

    def back_e(u):
        h, c, rows = unit(u)
        na, nb, no, nc = path(h)

        @pl.when((z == na) | (z == nc))
        def _():
            remote(mem.at[h, rows], land3.at[h, rows], s0.at[u], r3.at[u], y, nb).wait_recv()
            pref[h, rows] = land3[h, rows].astype(BF16)

    def sends_done(u, _):
        h, c, rows = unit(u)
        na, nb, no, nc = path(h)

        def done(sem):
            remote(mem.at[h, rows], land1.at[h, rows], sem, r1.at[u], y, nb).wait_send()

        @pl.when((z != no) | (y < NY - 1))
        def _():
            done(s0.at[u])

        @pl.when((z == nb) | (z == no))
        def _():
            done(s1.at[u])

        @pl.when(z == no)
        def _():
            done(s2.at[u])

        @pl.when((z == no) & (y == NY - 1))
        def _():
            for j in range(NZ):
                @pl.when((c != NY - 1) | (z != j))
                def _():
                    remote(
                        mem.at[h, pl.ds(0, STEP)], fin.at[h], sf.at[u * NZ + j], rf.at[h], y, nb
                    ).wait_send()
        return 0

    row_id = lax.broadcasted_iota(jnp.int32, (TILE, TILE), 0)
    col_id = lax.broadcasted_iota(jnp.int32, (TILE, TILE), 1)
    lane_id = lax.broadcasted_iota(jnp.int32, (TILE, 128), 1)

    def attend(h, i):
        q = qs[h, i * TILE:(i + 1) * TILE, :]
        bcol = column(cols1, i * TILE, TILE, h, H)
        total = jnp.zeros((TILE, DV), F32)
        den = jnp.zeros((TILE, 1), F32)
        for j in range(i + 1):
            span = slice(j * TILE, (j + 1) * TILE)
            s = lax.dot_general(q, ks[h, span, :], (((1,), (1,)), ((), ())), preferred_element_type=F32)
            p = jnp.exp(arow[pl.ds(h, 1), span] - bcol) * s
            if j == i:
                p = jnp.where(row_id >= col_id, p, 0.0)
            den = den + jnp.sum(p, axis=1, keepdims=True)
            total = total + jnp.dot(p.astype(BF16), vs[h, span, :], preferred_element_type=F32)
        acc[h, i * TILE:(i + 1) * TILE, :] = total
        at = slice(i * TILE, (i + 1) * TILE)
        dens[at, :] = jnp.where(lane_id == h, den, dens[at, :])

    def finish(h):
        def tile(i, _):
            at = pl.ds(pl.multiple_of(i * TILE, TILE), TILE)
            q = qs[h, at, :]
            carried_term = jnp.dot(q, pref[h], preferred_element_type=F32)
            qn = jnp.sum(q.astype(F32) * pnorm[pl.ds(h, 1), :], axis=1, keepdims=True)
            start = pl.multiple_of(i * TILE, TILE)
            w1 = column(cols2, start, TILE, h, 0)
            w2 = column(cols2, start, TILE, h, H)
            floor = column(cols2, start, TILE, h, 2 * H)
            den = column(dens, start, TILE, h, 0)
            bottom = jnp.maximum(jnp.abs(w1 * qn + w2 * den), floor)
            vs[h, at, :] = ((w1 * carried_term + w2 * acc[h, at, :]) / bottom).astype(BF16)
            return 0

        lax.fori_loop(0, LEN // TILE, tile, 0)
        pltpu.make_async_copy(
            vs.at[h], out_hbm.at[:, pl.ds(pl.multiple_of(h * DV, DV), DV)], out_sem.at[h]
        ).start()

    lag_o = LAG_O + LAG_Y * y
    lag_b = lag_o + LAG_B
    lag_e = lag_b + LAG_E

    def guarded(fn, u):
        @pl.when((u >= 0) & (u < UNITS))
        def _():
            fn(jnp.clip(u, 0, UNITS - 1))

    normals()

    def main(hh, _):
        for c in range(PIECES):
            v = hh * PIECES + c
            guarded(gather_b, v)
            guarded(own_o, v - lag_o)
            guarded(back_b, v - lag_b)
            guarded(back_e, v - lag_e)

            @pl.when(hh < H)
            def _():
                h = jnp.minimum(hh, H - 1)
                if c == 0:
                    pltpu.make_async_copy(q_hbm.at[:, 0:DQK], qs.at[h], in_sem.at[2 * H + h]).wait()
                attend(h, c)
        hf = hh - (lag_e + PIECES - 1) // PIECES

        @pl.when((hf >= 0) & (hf < H))
        def _():
            finish(jnp.clip(hf, 0, H - 1))
        return 0

    max_lag = LAG_O + LAG_Y * (NY - 1) + LAG_B + LAG_E
    lax.fori_loop(0, H + (max_lag + PIECES - 1) // PIECES, main, 0)

    def last(h, _):
        na, nb, no, nc = path(h)

        @pl.when((y != NY - 1) | (z != no))
        def _():
            remote(mem.at[h, pl.ds(0, STEP)], fin.at[h], s0.at[0], rf.at[h], y, nb).wait_recv()
        finm_ref[h] = fin[h]
        pltpu.make_async_copy(vs.at[h], out_hbm.at[:, 0:DV], out_sem.at[h]).wait()
        return 0

    lax.fori_loop(0, H, last, 0)
    lax.fori_loop(0, UNITS, sends_done, 0)
    spread_done(stats, sstat, rstat)
    spread_done(norms, snorm, rnorm)


def shards(query_matrix, key_vectors, value_vectors, input_gate, forget_gate):
    vmem = pl.BlockSpec(memory_space=pltpu.VMEM)
    hbm = pl.BlockSpec(memory_space=pl.ANY)
    dma = pltpu.SemaphoreType.DMA
    ctx = NY * NZ
    hidden, final_memory, small = pl.pallas_call(
        kernel,
        out_shape=(
            jax.ShapeDtypeStruct((LEN, H * DV), BF16),
            jax.ShapeDtypeStruct((H, DQK // ctx, DV), F32),
            jax.ShapeDtypeStruct((2 * H, 128), F32),
        ),
        in_specs=[hbm, hbm, hbm, vmem, vmem],
        out_specs=(hbm, vmem, vmem),
        scratch_shapes=[
            pltpu.VMEM((H, LEN, DQK), BF16),
            pltpu.VMEM((H, LEN, DQK), BF16),
            pltpu.VMEM((H, LEN, DV), BF16),
            pltpu.VMEM((H, DQK, DV), F32),
            pltpu.VMEM((H, DQK, DV), F32),
            pltpu.VMEM((H, DQK, DV), F32),
            pltpu.VMEM((H, DQK, DV), F32),
            pltpu.VMEM((H, DQK, DV), F32),
            pltpu.VMEM((H, LEN, DV), F32),
            pltpu.VMEM((H, DQK, DV), BF16),
            pltpu.VMEM((LEN, 128), F32),
            pltpu.VMEM((LEN, 128), F32),
            pltpu.VMEM((LEN, 128), F32),
            pltpu.VMEM((128, LEN), F32),
            pltpu.VMEM((H, LEN), F32),
            pltpu.VMEM((2, H, LEN), F32),
            pltpu.VMEM((NCOEF, H, DV), F32),
            pltpu.VMEM((ctx, 2 * H, 128), F32),
            pltpu.VMEM((ctx, H, DQK), F32),
            pltpu.VMEM((H, DQK), F32),
            pltpu.VMEM((H, DQK // ctx, DV), F32),
            dma((3 * H,)),
            dma((H,)),
            dma((UNITS,)),
            dma((UNITS,)),
            dma((UNITS,)),
            dma((UNITS,)),
            dma((UNITS,)),
            dma((UNITS,)),
            dma((UNITS * NZ,)),
            dma((H,)),
            dma((ctx,)),
            dma((ctx,)),
            dma((ctx,)),
            dma((ctx,)),
            dma((1,)),
        ],
        compiler_params=pltpu.CompilerParams(
            collective_id=0, has_side_effects=True, vmem_limit_bytes=67_000_000
        ),
        name="mlstm_cell",
    )(query_matrix, key_vectors, value_vectors, input_gate, forget_gate)
    return (hidden, final_memory, small[0:H, 0:DQK // ctx], small[H:2 * H, 0])


def solution(mesh):
    split = Mesh(mesh.devices.reshape(NY, NZ, mesh.shape["seq"]), ("ctx_0", "ctx_1", "seq"))
    return jax.shard_map(
        shards,
        mesh=split,
        in_specs=(
            P(SEQ_CTX, None),
            P(SEQ_CTX, None),
            P(SEQ_CTX, None),
            P(None, SEQ_CTX),
            P(None, SEQ_CTX),
        ),
        out_specs=(P(SEQ_CTX, None), P("seq", CTX, None), P("seq", CTX), P("seq")),
        check_vma=False,
    )
```

```python
import functools

import jax
import jax.numpy as jnp
from jax import lax
from jax.experimental import pallas as pl
from jax.experimental.pallas import tpu as pltpu
from jax.sharding import Mesh
from jax.sharding import PartitionSpec as P

H = 8
DQK = 256
DV = 512
LEN = 1024
NY = 4
NZ = 4
CTX = ("ctx_0", "ctx_1")
SEQ_CTX = ("seq", "ctx_0", "ctx_1")
NEG = -1e30
F32 = jnp.float32
BF16 = jnp.bfloat16
MESH = pl.DeviceIdType.MESH

PATHS = {
    1: (2, 1, 0, 3),
    2: (2, 3, 0, 1),
    3: (3, 2, 1, 0),
    4: (0, 1, 2, 3),
    5: (1, 2, 3, 0),
    6: (1, 0, 3, 2),
}
KINDS = (2, 5, 1, 3, 5, 4, 1, 6)
ZC = {1: (1, 1, 0), 2: (0, 1, 0), 3: (0, 0, 0), 4: (1, 1, 0), 5: (0, 0, 0), 6: (1, 0, 0)}
ZB = {1: (0, 1, 0), 2: (0, 1, 1), 3: (0, 1, 1), 4: (0, 0, 0), 5: (0, 0, 1), 6: (0, 0, 0)}
PO = {1: (0, 0, 0), 2: (0, 0, 0), 3: (0, 0, 1), 4: (1, 0, 0), 5: (1, 0, 1), 6: (1, 0, 1)}
PB_A = {1: 0, 2: 1, 3: 0, 4: 1, 5: 1, 6: 0}
ZA_B = {1: 1, 2: 0, 3: 1, 4: 0, 5: 0, 6: 1}

PIECES = 4
ROWS = DQK // PIECES
UNITS = H * PIECES
LAG_O = 15
LAG_Y = 4
LAG_B = 12
LAG_E = 9
LAG_A = 0
LEAD = 17
EARLY = 8
NCOEF = 22
TILE = 256


def pick(h, values):
    out = jnp.int32(values[-1])
    for i in range(len(values) - 1):
        out = jnp.where(h == i, jnp.int32(values[i]), out)
    return out


def kernel(
    q_hbm, k_hbm, v_hbm, gate_ref, forget_ref,
    out_hbm, finm_ref, fins_ref,
    qs, ks, vs, mem, land1, land2, land3, send1, acc, pref,
    cols1, cols2, dens, rows_tmp, arow, rowst, ctab, stats, norms, pnorm, fin,
    in_sem, out_sem, r1, r2, r3, s0, s1, s2, sf, rf, rstat, rnorm, sstat, snorm, loc_sem,
):
    y = lax.axis_index("ctx_0")
    z = lax.axis_index("ctx_1")
    me = y * NZ + z

    def remote(src, dst, ss, rs, yy, zz):
        return pltpu.make_async_remote_copy(
            src_ref=src, dst_ref=dst, send_sem=ss, recv_sem=rs,
            device_id={"ctx_0": yy, "ctx_1": zz}, device_id_type=MESH,
        )

    def load(hbm, dst, h, width, sem):
        return pltpu.make_async_copy(hbm.at[:, h * width:(h + 1) * width], dst.at[h], sem)

    loads = []
    for h in range(H):
        loads.append((
            load(k_hbm, ks, h, DQK, in_sem.at[h]),
            load(v_hbm, vs, h, DV, in_sem.at[H + h]),
            load(q_hbm, qs, h, DQK, in_sem.at[2 * H + h]),
        ))
    for h in range(H):
        loads[h][0].start()
        loads[h][1].start()
    for h in range(H):
        loads[h][2].start()

    barrier = pltpu.get_barrier_semaphore()

    def greet(i, _):
        peer = lax.rem(me + i, NY * NZ)
        pl.semaphore_signal(
            barrier, inc=1,
            device_id={"ctx_0": peer // NZ, "ctx_1": lax.rem(peer, NZ)}, device_id_type=MESH,
        )
        return 0

    lax.fori_loop(1, NY * NZ, greet, 0)

    lane = lax.broadcasted_iota(jnp.int32, (H, LEN), 1)
    f = forget_ref[...]
    cum = jnp.minimum(f, 0.0) - jnp.log1p(jnp.exp(-jnp.abs(f)))
    for s in (1, 2, 4, 8, 16, 32, 64, 128, 256, 512):
        cum = cum + jnp.where(lane >= s, pltpu.roll(cum, s, 1), 0.0)
    a = gate_ref[...] - cum
    b0 = a
    for s in (1, 2, 4, 8, 16, 32, 64, 128, 256, 512):
        b0 = jnp.maximum(b0, jnp.where(lane >= s, pltpu.roll(b0, s, 1), NEG))
    arow[...] = a
    rowst[0] = b0
    rowst[1] = cum
    amax = b0[:, LEN - 1:LEN]
    rows_tmp[...] = jnp.zeros_like(rows_tmp)
    rows_tmp[0:H, :] = jnp.exp(a - amax)
    rows_tmp[H:2 * H, :] = b0
    cols1[...] = rows_tmp[...].T
    decay = cum[:, LEN - 1:LEN]
    stats[me, 0:H] = jnp.broadcast_to(decay + amax, (H, 128))
    stats[me, H:2 * H] = jnp.broadcast_to(decay, (H, 128))
    dens[...] = jnp.zeros_like(dens)

    pl.semaphore_wait(barrier, NY * NZ - 1)

    def spread(table, ss, rs):
        def one(i, _):
            peer = lax.rem(me + i, NY * NZ)
            remote(table.at[me], table.at[me], ss.at[peer], rs.at[me], peer // NZ, lax.rem(peer, NZ)).start()
            return 0
        lax.fori_loop(1, NY * NZ, one, 0)

    def gathered(table, ss, rs):
        def one(i, _):
            peer = lax.rem(me + i, NY * NZ)
            remote(table.at[peer], table.at[peer], ss.at[peer], rs.at[peer], y, z).wait_recv()
            return 0
        lax.fori_loop(1, NY * NZ, one, 0)

    def spread_done(table, ss, rs):
        def one(i, _):
            peer = lax.rem(me + i, NY * NZ)
            remote(table.at[me], table.at[me], ss.at[peer], rs.at[me], y, z).wait_send()
            return 0
        lax.fori_loop(1, NY * NZ, one, 0)

    spread(stats, sstat, rstat)

    def path(h):
        return tuple(pick(h, [PATHS[k][i] for k in KINDS]) for i in range(4))

    def unit(u):
        h = u // PIECES
        c = u - h * PIECES
        return h, c, pl.ds(pl.multiple_of(c * ROWS, ROWS), ROWS)

    def column(table, start, size, h, base):
        x = pltpu.roll(table[pl.ds(start, size), :], lax.rem(128 - h, 128), 1)
        return x[:, base:base + 1]

    def summarize(h, _):
        pltpu.make_async_copy(k_hbm.at[:, 0:DQK], ks.at[h], in_sem.at[h]).wait()
        pltpu.make_async_copy(v_hbm.at[:, 0:DV], vs.at[h], in_sem.at[H + h]).wait()
        scaled = ks[h].astype(F32) * column(cols1, 0, LEN, h, 0)
        norms[me, pl.ds(h, 1), :] = jnp.sum(scaled, axis=0, keepdims=True)
        mem[h] = lax.dot_general(
            scaled.astype(BF16), vs[h], (((0,), (0,)), ((), ())), preferred_element_type=F32
        )
        return 0

    def first_send(u):
        h, c, rows = unit(u)
        na, nb, no, nc = path(h)

        @pl.when(z == na)
        def _():
            remote(mem.at[h, rows], land1.at[h, rows], s0.at[u], r1.at[u], y, nb).start()

        @pl.when(z == nc)
        def _():
            remote(mem.at[h, rows], land2.at[h, rows], s0.at[u], r2.at[u], y, no).start()

    def begin(h, _):
        summarize(h, 0)
        for c in range(PIECES):
            @pl.when(h * PIECES + c < LEAD)
            def _():
                first_send(h * PIECES + c)
        return 0

    lax.fori_loop(0, EARLY, begin, 0)

    gathered(stats, sstat, rstat)
    sub = lax.broadcasted_iota(jnp.int32, (H, 128), 0)

    def by_head(table):
        out = jnp.zeros((H, 128), F32)
        for h in range(H):
            if table[KINDS[h]] != 0:
                out = jnp.where(sub == h, 1.0, out)
        return out > 0.5

    total = jnp.zeros((H, 128), F32)
    before = jnp.zeros((H, 128), F32)
    top_row = jnp.full((H, 128), NEG, F32)
    top_me = jnp.full((H, 128), NEG, F32)
    top_all = jnp.full((H, 128), NEG, F32)
    logs = []
    for i in range(NY * NZ):
        before = jnp.where(me == i, total, before)
        dec = stats[i, H:2 * H]
        total = total + dec
        w = stats[i, 0:H] - total
        logs.append(w)
        top_row = jnp.maximum(top_row, jnp.where(i < y * NZ, w, NEG))
        top_me = jnp.maximum(top_me, jnp.where(i < me, w, NEG))
        top_all = jnp.maximum(top_all, w)
    here = []
    for j in range(NZ):
        w = logs[j]
        for r in range(1, NY):
            w = jnp.where(y == r, logs[r * NZ + j], w)
        here.append(w)

    def node(i):
        out = here[0]
        for j in range(1, NZ):
            mask = by_head({k: int(PATHS[k][i] == j) for k in PATHS})
            out = jnp.where(mask, here[j], out)
        return out

    l_a, l_b, l_o, l_c = (node(i) for i in range(4))
    l_ab = jnp.maximum(l_a, l_b)
    coefs = [jnp.exp(l_a - l_ab), jnp.exp(l_b - l_ab)]

    def union(base, parts):
        top = base
        for value, mask in parts:
            top = jnp.maximum(top, value if mask is None else jnp.where(mask, value, NEG))
        out = [jnp.exp(base - top)]
        for value, mask in parts:
            e = jnp.exp(value - top)
            out.append(e if mask is None else jnp.where(mask, e, 0.0))
        return top, out

    coefs += union(top_row, [(l_ab, None), (l_o, None), (l_c, None)])[1]
    tops = {}
    for name, table in (("c", ZC), ("b", ZB), ("o", PO)):
        masks = [by_head({k: table[k][i] for k in table}) for i in range(3)]
        tops[name], cs = union(top_row, list(zip((l_ab, l_o, l_c), masks)))
        coefs += cs
    coefs += union(tops["b"], [(l_a, by_head(PB_A))])[1]
    coefs += union(tops["b"], [(l_b, by_head(ZA_B))])[1]
    for i, cf in enumerate(coefs):
        ctab[i] = jnp.concatenate([cf] * (DV // 128), axis=1)

    carried = top_me + before
    prefix_top = carried[:, 0:1]
    b0 = rowst[0]
    cum = rowst[1]
    b = jnp.maximum(prefix_top, b0)
    rows_tmp[0:H, :] = jnp.exp(prefix_top - b) * (1.0 / 16.0)
    rows_tmp[H:2 * H, :] = jnp.exp(b0 - b) * (1.0 / 16.0)
    rows_tmp[2 * H:3 * H, :] = jnp.exp(-(cum + b))
    cols2[...] = rows_tmp[...].T
    fins_ref[H:2 * H, :] = top_all + total

    def normals():
        gathered(norms, snorm, rnorm)
        tot = jnp.zeros((H, DQK), F32)
        mine = jnp.zeros((H, DQK), F32)
        for i in range(NY * NZ):
            n = norms[i]
            w_all = jnp.exp(logs_ref(i) - top_all[:, 0:1])
            w_me = jnp.where(i < me, jnp.exp(logs_ref(i) - top_me[:, 0:1]), 0.0)
            tot = tot + w_all * n
            mine = mine + w_me * n
        pnorm[0:H, :] = mine
        turned = pltpu.roll(tot, lax.rem(DQK - me * (DQK // (NY * NZ)), DQK), 1)
        fins_ref[0:H, :] = turned[:, 0:128]

    def logs_ref(i):
        return logs[i][:, 0:1]

    def coef(i, h):
        return ctab[i, pl.ds(h, 1), :]

    STEP = 16

    def gather_b(u):
        h, c, rows = unit(u)
        na, nb, no, nc = path(h)

        @pl.when(z == nb)
        def _():
            remote(mem.at[h, rows], land1.at[h, rows], s0.at[u], r1.at[u], y, no).wait_recv()
            for t in range(ROWS // STEP):
                part = pl.ds(pl.multiple_of(c * ROWS + t * STEP, STEP), STEP)
                send1[h, part] = coef(0, h) * land1[h, part] + coef(1, h) * mem[h, part]
            remote(send1.at[h, rows], land1.at[h, rows], s0.at[u], r1.at[u], y, no).start()

    def own_o(u):
        h, c, rows = unit(u)
        na, nb, no, nc = path(h)

        @pl.when(z == no)
        def _():
            remote(mem.at[h, rows], land1.at[h, rows], s0.at[u], r1.at[u], y, nb).wait_recv()
            remote(mem.at[h, rows], land2.at[h, rows], s0.at[u], r2.at[u], y, nb).wait_recv()

            @pl.when(y == 0)
            def _():
                land3[h, rows] = jnp.zeros((ROWS, DV), F32)

            @pl.when(y > 0)
            def _():
                remote(mem.at[h, rows], land3.at[h, rows], s0.at[u], r3.at[u], y, nb).wait_recv()

            for t in range(ROWS // STEP):
                part = pl.ds(pl.multiple_of(c * ROWS + t * STEP, STEP), STEP)
                r = land3[h, part]
                xb = land1[h, part]
                xc = land2[h, part]
                mo = mem[h, part]

                def mix(i):
                    return coef(i, h) * r + coef(i + 1, h) * xb + coef(i + 2, h) * mo + coef(i + 3, h) * xc

                send1[h, part] = mix(2)
                land2[h, part] = mix(6)
                land1[h, part] = mix(10)
                pref[h, part] = mix(14).astype(BF16)

            @pl.when(y < NY - 1)
            def _():
                remote(send1.at[h, rows], land3.at[h, rows], s0.at[u], r3.at[u], y + 1, z).start()

            remote(land1.at[h, rows], land3.at[h, rows], s1.at[u], r3.at[u], y, nb).start()
            remote(land2.at[h, rows], land3.at[h, rows], s2.at[u], r3.at[u], y, nc).start()

            @pl.when(y == NY - 1)
            def _():
                for j in range(NZ):
                    part = pl.ds(pl.multiple_of(c * ROWS + j * STEP, STEP), STEP)

                    @pl.when((c != NY - 1) | (z != j))
                    def _():
                        remote(send1.at[h, part], fin.at[h], sf.at[u * NZ + j], rf.at[h], c, j).start()

                    @pl.when((c == NY - 1) & (z == j))
                    def _():
                        fin[h] = send1[h, part]

    def back_b(u):
        h, c, rows = unit(u)
        na, nb, no, nc = path(h)

        @pl.when(z == nb)
        def _():
            remote(mem.at[h, rows], land3.at[h, rows], s0.at[u], r3.at[u], y, no).wait_recv()
            for t in range(ROWS // STEP):
                part = pl.ds(pl.multiple_of(c * ROWS + t * STEP, STEP), STEP)
                zb = land3[h, part]
                pref[h, part] = (coef(18, h) * zb + coef(19, h) * land1[h, part]).astype(BF16)
                land3[h, part] = coef(20, h) * zb + coef(21, h) * mem[h, part]
            remote(land3.at[h, rows], land3.at[h, rows], s1.at[u], r3.at[u], y, na).start()

    def back_e(u):
        h, c, rows = unit(u)
        na, nb, no, nc = path(h)

        @pl.when((z == na) | (z == nc))
        def _():
            remote(mem.at[h, rows], land3.at[h, rows], s0.at[u], r3.at[u], y, nb).wait_recv()
            pref[h, rows] = land3[h, rows].astype(BF16)

    def sends_done(u, _):
        h, c, rows = unit(u)
        na, nb, no, nc = path(h)

        def done(sem):
            remote(mem.at[h, rows], land1.at[h, rows], sem, r1.at[u], y, nb).wait_send()

        @pl.when((z != no) | (y < NY - 1))
        def _():
            done(s0.at[u])

        @pl.when((z == nb) | (z == no))
        def _():
            done(s1.at[u])

        @pl.when(z == no)
        def _():
            done(s2.at[u])

        @pl.when((z == no) & (y == NY - 1))
        def _():
            for j in range(NZ):
                @pl.when((c != NY - 1) | (z != j))
                def _():
                    remote(
                        mem.at[h, pl.ds(0, STEP)], fin.at[h], sf.at[u * NZ + j], rf.at[h], y, nb
                    ).wait_send()
        return 0

    row_id = lax.broadcasted_iota(jnp.int32, (TILE, TILE), 0)
    col_id = lax.broadcasted_iota(jnp.int32, (TILE, TILE), 1)
    lane_id = lax.broadcasted_iota(jnp.int32, (TILE, 128), 1)

    def attend(h, i):
        q = qs[h, i * TILE:(i + 1) * TILE, :]
        bcol = column(cols1, i * TILE, TILE, h, H)
        total = jnp.zeros((TILE, DV), F32)
        den = jnp.zeros((TILE, 1), F32)
        for j in range(i + 1):
            span = slice(j * TILE, (j + 1) * TILE)
            s = lax.dot_general(q, ks[h, span, :], (((1,), (1,)), ((), ())), preferred_element_type=F32)
            p = jnp.exp(arow[pl.ds(h, 1), span] - bcol) * s
            if j == i:
                p = jnp.where(row_id >= col_id, p, 0.0)
            den = den + jnp.sum(p, axis=1, keepdims=True)
            total = total + jnp.dot(p.astype(BF16), vs[h, span, :], preferred_element_type=F32)
        acc[h, i * TILE:(i + 1) * TILE, :] = total
        at = slice(i * TILE, (i + 1) * TILE)
        dens[at, :] = jnp.where(lane_id == h, den, dens[at, :])

    def finish(h):
        def tile(i, _):
            at = pl.ds(pl.multiple_of(i * TILE, TILE), TILE)
            q = qs[h, at, :]
            carried_term = jnp.dot(q, pref[h], preferred_element_type=F32)
            qn = jnp.sum(q.astype(F32) * pnorm[pl.ds(h, 1), :], axis=1, keepdims=True)
            start = pl.multiple_of(i * TILE, TILE)
            w1 = column(cols2, start, TILE, h, 0)
            w2 = column(cols2, start, TILE, h, H)
            floor = column(cols2, start, TILE, h, 2 * H)
            den = column(dens, start, TILE, h, 0)
            bottom = jnp.maximum(jnp.abs(w1 * qn + w2 * den), floor)
            vs[h, at, :] = ((w1 * carried_term + w2 * acc[h, at, :]) / bottom).astype(BF16)
            return 0

        lax.fori_loop(0, LEN // TILE, tile, 0)
        pltpu.make_async_copy(
            vs.at[h], out_hbm.at[:, pl.ds(pl.multiple_of(h * DV, DV), DV)], out_sem.at[h]
        ).start()

    lag_o = LAG_O + LAG_Y * y
    lag_b = lag_o + LAG_B
    lag_e = lag_b + LAG_E

    def guarded(fn, u):
        @pl.when((u >= 0) & (u < UNITS))
        def _():
            fn(jnp.clip(u, 0, UNITS - 1))

    def main(hh, _):
        @pl.when(hh + EARLY < H)
        def _():
            summarize(jnp.minimum(hh + EARLY, H - 1), 0)

        @pl.when(hh == H - EARLY)
        def _():
            spread(norms, snorm, rnorm)

        @pl.when(hh == H - EARLY + 1)
        def _():
            normals()

        for c in range(PIECES):
            v = hh * PIECES + c
            guarded(first_send, v + LEAD)
            guarded(gather_b, v)
            guarded(own_o, v - lag_o)
            guarded(back_b, v - lag_b)
            guarded(back_e, v - lag_e)

            @pl.when((hh >= LAG_A) & (hh < H + LAG_A))
            def _():
                h = jnp.clip(hh - LAG_A, 0, H - 1)
                if c == 0:
                    pltpu.make_async_copy(q_hbm.at[:, 0:DQK], qs.at[h], in_sem.at[2 * H + h]).wait()
                attend(h, c)
        hf = hh - jnp.maximum((lag_e + PIECES - 1) // PIECES, max(H - EARLY + 1, LAG_A))

        @pl.when((hf >= 0) & (hf < H))
        def _():
            finish(jnp.clip(hf, 0, H - 1))
        return 0

    max_lag = LAG_O + LAG_Y * (NY - 1) + LAG_B + LAG_E
    lax.fori_loop(0, H + max((max_lag + PIECES - 1) // PIECES, H - EARLY + 1, LAG_A), main, 0)

    def last(h, _):
        na, nb, no, nc = path(h)

        @pl.when((y != NY - 1) | (z != no))
        def _():
            remote(mem.at[h, pl.ds(0, STEP)], fin.at[h], s0.at[0], rf.at[h], y, nb).wait_recv()
        finm_ref[h] = fin[h]
        pltpu.make_async_copy(vs.at[h], out_hbm.at[:, 0:DV], out_sem.at[h]).wait()
        return 0

    lax.fori_loop(0, H, last, 0)
    lax.fori_loop(0, UNITS, sends_done, 0)
    spread_done(stats, sstat, rstat)
    spread_done(norms, snorm, rnorm)


def shards(query_matrix, key_vectors, value_vectors, input_gate, forget_gate):
    vmem = pl.BlockSpec(memory_space=pltpu.VMEM)
    hbm = pl.BlockSpec(memory_space=pl.ANY)
    dma = pltpu.SemaphoreType.DMA
    ctx = NY * NZ
    hidden, final_memory, small = pl.pallas_call(
        kernel,
        out_shape=(
            jax.ShapeDtypeStruct((LEN, H * DV), BF16),
            jax.ShapeDtypeStruct((H, DQK // ctx, DV), F32),
            jax.ShapeDtypeStruct((2 * H, 128), F32),
        ),
        in_specs=[hbm, hbm, hbm, vmem, vmem],
        out_specs=(hbm, vmem, vmem),
        scratch_shapes=[
            pltpu.VMEM((H, LEN, DQK), BF16),
            pltpu.VMEM((H, LEN, DQK), BF16),
            pltpu.VMEM((H, LEN, DV), BF16),
            pltpu.VMEM((H, DQK, DV), F32),
            pltpu.VMEM((H, DQK, DV), F32),
            pltpu.VMEM((H, DQK, DV), F32),
            pltpu.VMEM((H, DQK, DV), F32),
            pltpu.VMEM((H, DQK, DV), F32),
            pltpu.VMEM((H, LEN, DV), F32),
            pltpu.VMEM((H, DQK, DV), BF16),
            pltpu.VMEM((LEN, 128), F32),
            pltpu.VMEM((LEN, 128), F32),
            pltpu.VMEM((LEN, 128), F32),
            pltpu.VMEM((128, LEN), F32),
            pltpu.VMEM((H, LEN), F32),
            pltpu.VMEM((2, H, LEN), F32),
            pltpu.VMEM((NCOEF, H, DV), F32),
            pltpu.VMEM((ctx, 2 * H, 128), F32),
            pltpu.VMEM((ctx, H, DQK), F32),
            pltpu.VMEM((H, DQK), F32),
            pltpu.VMEM((H, DQK // ctx, DV), F32),
            dma((3 * H,)),
            dma((H,)),
            dma((UNITS,)),
            dma((UNITS,)),
            dma((UNITS,)),
            dma((UNITS,)),
            dma((UNITS,)),
            dma((UNITS,)),
            dma((UNITS * NZ,)),
            dma((H,)),
            dma((ctx,)),
            dma((ctx,)),
            dma((ctx,)),
            dma((ctx,)),
            dma((1,)),
        ],
        compiler_params=pltpu.CompilerParams(
            collective_id=0, has_side_effects=True, vmem_limit_bytes=67_000_000
        ),
        name="mlstm_cell",
    )(query_matrix, key_vectors, value_vectors, input_gate, forget_gate)
    return (hidden, final_memory, small[0:H, 0:DQK // ctx], small[H:2 * H, 0])


def solution(mesh):
    split = Mesh(mesh.devices.reshape(NY, NZ, mesh.shape["seq"]), ("ctx_0", "ctx_1", "seq"))
    return jax.shard_map(
        shards,
        mesh=split,
        in_specs=(
            P(SEQ_CTX, None),
            P(SEQ_CTX, None),
            P(SEQ_CTX, None),
            P(None, SEQ_CTX),
            P(None, SEQ_CTX),
        ),
        out_specs=(P(SEQ_CTX, None), P("seq", CTX, None), P("seq", CTX), P("seq")),
        check_vma=False,
    )
```

```python
import functools

import jax
import jax.numpy as jnp
from jax import lax
from jax.experimental import pallas as pl
from jax.experimental.pallas import tpu as pltpu
from jax.sharding import Mesh
from jax.sharding import PartitionSpec as P

H = 8
DQK = 256
DV = 512
LEN = 1024
NY = 4
NZ = 4
CTX = ("ctx_0", "ctx_1")
SEQ_CTX = ("seq", "ctx_0", "ctx_1")
NEG = -1e30
F32 = jnp.float32
BF16 = jnp.bfloat16
MESH = pl.DeviceIdType.MESH

PATHS = {
    1: (2, 1, 0, 3),
    2: (2, 3, 0, 1),
    3: (3, 2, 1, 0),
    4: (0, 1, 2, 3),
    5: (1, 2, 3, 0),
    6: (1, 0, 3, 2),
}
KINDS = (2, 5, 1, 3, 5, 4, 1, 6)
ZC = {1: (1, 1, 0), 2: (0, 1, 0), 3: (0, 0, 0), 4: (1, 1, 0), 5: (0, 0, 0), 6: (1, 0, 0)}
ZB = {1: (0, 1, 0), 2: (0, 1, 1), 3: (0, 1, 1), 4: (0, 0, 0), 5: (0, 0, 1), 6: (0, 0, 0)}
PO = {1: (0, 0, 0), 2: (0, 0, 0), 3: (0, 0, 1), 4: (1, 0, 0), 5: (1, 0, 1), 6: (1, 0, 1)}
PB_A = {1: 0, 2: 1, 3: 0, 4: 1, 5: 1, 6: 0}
ZA_B = {1: 1, 2: 0, 3: 1, 4: 0, 5: 0, 6: 1}

PIECES = 4
ROWS = DQK // PIECES
UNITS = H * PIECES
LAG_O = 15
LAG_Y = 4
LAG_B = 12
LAG_E = 9
LAG_A = 0
LEAD = 17
EARLY = 8
NCOEF = 22
TILE = 256


def pick(h, values):
    out = jnp.int32(values[-1])
    for i in range(len(values) - 1):
        out = jnp.where(h == i, jnp.int32(values[i]), out)
    return out


def kernel(
    q_hbm, k_hbm, v_hbm, gate_ref, forget_ref,
    vs, finm_ref, fins_ref,
    qs, ks, mem, land1, land2, land3, send1, acc, pref,
    cols1, cols2, dens, rows_tmp, arow, rowst, ctab, stats, norms, pnorm, fin,
    in_sem, r1, r2, r3, s0, s1, s2, sf, rf, rstat, rnorm, sstat, snorm, loc_sem,
):
    y = lax.axis_index("ctx_0")
    z = lax.axis_index("ctx_1")
    me = y * NZ + z

    def remote(src, dst, ss, rs, yy, zz):
        return pltpu.make_async_remote_copy(
            src_ref=src, dst_ref=dst, send_sem=ss, recv_sem=rs,
            device_id={"ctx_0": yy, "ctx_1": zz}, device_id_type=MESH,
        )

    def load(hbm, dst, h, width, sem):
        return pltpu.make_async_copy(hbm.at[:, h * width:(h + 1) * width], dst.at[h], sem)

    loads = []
    for h in range(H):
        loads.append((
            load(k_hbm, ks, h, DQK, in_sem.at[h]),
            load(v_hbm, vs, h, DV, in_sem.at[H + h]),
            load(q_hbm, qs, h, DQK, in_sem.at[2 * H + h]),
        ))
    for h in range(H):
        loads[h][0].start()
        loads[h][1].start()
    for h in range(H):
        loads[h][2].start()

    barrier = pltpu.get_barrier_semaphore()

    def greet(i, _):
        peer = lax.rem(me + i, NY * NZ)
        pl.semaphore_signal(
            barrier, inc=1,
            device_id={"ctx_0": peer // NZ, "ctx_1": lax.rem(peer, NZ)}, device_id_type=MESH,
        )
        return 0

    lax.fori_loop(1, NY * NZ, greet, 0)

    lane = lax.broadcasted_iota(jnp.int32, (H, LEN), 1)
    f = forget_ref[...]
    cum = jnp.minimum(f, 0.0) - jnp.log1p(jnp.exp(-jnp.abs(f)))
    for s in (1, 2, 4, 8, 16, 32, 64, 128, 256, 512):
        cum = cum + jnp.where(lane >= s, pltpu.roll(cum, s, 1), 0.0)
    a = gate_ref[...] - cum
    b0 = a
    for s in (1, 2, 4, 8, 16, 32, 64, 128, 256, 512):
        b0 = jnp.maximum(b0, jnp.where(lane >= s, pltpu.roll(b0, s, 1), NEG))
    arow[...] = a
    rowst[0] = b0
    rowst[1] = cum
    amax = b0[:, LEN - 1:LEN]
    rows_tmp[...] = jnp.zeros_like(rows_tmp)
    rows_tmp[0:H, :] = jnp.exp(a - amax)
    rows_tmp[H:2 * H, :] = b0
    cols1[...] = rows_tmp[...].T
    decay = cum[:, LEN - 1:LEN]
    stats[me, 0:H] = jnp.broadcast_to(decay + amax, (H, 128))
    stats[me, H:2 * H] = jnp.broadcast_to(decay, (H, 128))
    dens[...] = jnp.zeros_like(dens)

    pl.semaphore_wait(barrier, NY * NZ - 1)

    def spread(table, ss, rs):
        def one(i, _):
            peer = lax.rem(me + i, NY * NZ)
            remote(table.at[me], table.at[me], ss.at[peer], rs.at[me], peer // NZ, lax.rem(peer, NZ)).start()
            return 0
        lax.fori_loop(1, NY * NZ, one, 0)

    def gathered(table, ss, rs):
        def one(i, _):
            peer = lax.rem(me + i, NY * NZ)
            remote(table.at[peer], table.at[peer], ss.at[peer], rs.at[peer], y, z).wait_recv()
            return 0
        lax.fori_loop(1, NY * NZ, one, 0)

    def spread_done(table, ss, rs):
        def one(i, _):
            peer = lax.rem(me + i, NY * NZ)
            remote(table.at[me], table.at[me], ss.at[peer], rs.at[me], y, z).wait_send()
            return 0
        lax.fori_loop(1, NY * NZ, one, 0)

    spread(stats, sstat, rstat)

    def path(h):
        return tuple(pick(h, [PATHS[k][i] for k in KINDS]) for i in range(4))

    def unit(u):
        h = u // PIECES
        c = u - h * PIECES
        return h, c, pl.ds(pl.multiple_of(c * ROWS, ROWS), ROWS)

    def column(table, start, size, h, base):
        x = pltpu.roll(table[pl.ds(start, size), :], lax.rem(128 - h, 128), 1)
        return x[:, base:base + 1]

    def summarize(h, _):
        pltpu.make_async_copy(k_hbm.at[:, 0:DQK], ks.at[h], in_sem.at[h]).wait()
        pltpu.make_async_copy(v_hbm.at[:, 0:DV], vs.at[h], in_sem.at[H + h]).wait()
        scaled = ks[h].astype(F32) * column(cols1, 0, LEN, h, 0)
        norms[me, pl.ds(h, 1), :] = jnp.sum(scaled, axis=0, keepdims=True)
        mem[h] = lax.dot_general(
            scaled.astype(BF16), vs[h], (((0,), (0,)), ((), ())), preferred_element_type=F32
        )
        return 0

    def first_send(u):
        h, c, rows = unit(u)
        na, nb, no, nc = path(h)

        @pl.when(z == na)
        def _():
            remote(mem.at[h, rows], land1.at[h, rows], s0.at[u], r1.at[u], y, nb).start()

        @pl.when(z == nc)
        def _():
            remote(mem.at[h, rows], land2.at[h, rows], s0.at[u], r2.at[u], y, no).start()

    def begin(h, _):
        summarize(h, 0)
        for c in range(PIECES):
            @pl.when(h * PIECES + c < LEAD)
            def _():
                first_send(h * PIECES + c)
        return 0

    lax.fori_loop(0, EARLY, begin, 0)

    gathered(stats, sstat, rstat)
    sub = lax.broadcasted_iota(jnp.int32, (H, 128), 0)

    def by_head(table):
        out = jnp.zeros((H, 128), F32)
        for h in range(H):
            if table[KINDS[h]] != 0:
                out = jnp.where(sub == h, 1.0, out)
        return out > 0.5

    total = jnp.zeros((H, 128), F32)
    before = jnp.zeros((H, 128), F32)
    top_row = jnp.full((H, 128), NEG, F32)
    top_me = jnp.full((H, 128), NEG, F32)
    top_all = jnp.full((H, 128), NEG, F32)
    logs = []
    for i in range(NY * NZ):
        before = jnp.where(me == i, total, before)
        dec = stats[i, H:2 * H]
        total = total + dec
        w = stats[i, 0:H] - total
        logs.append(w)
        top_row = jnp.maximum(top_row, jnp.where(i < y * NZ, w, NEG))
        top_me = jnp.maximum(top_me, jnp.where(i < me, w, NEG))
        top_all = jnp.maximum(top_all, w)
    here = []
    for j in range(NZ):
        w = logs[j]
        for r in range(1, NY):
            w = jnp.where(y == r, logs[r * NZ + j], w)
        here.append(w)

    def node(i):
        out = here[0]
        for j in range(1, NZ):
            mask = by_head({k: int(PATHS[k][i] == j) for k in PATHS})
            out = jnp.where(mask, here[j], out)
        return out

    l_a, l_b, l_o, l_c = (node(i) for i in range(4))
    l_ab = jnp.maximum(l_a, l_b)
    coefs = [jnp.exp(l_a - l_ab), jnp.exp(l_b - l_ab)]

    def union(base, parts):
        top = base
        for value, mask in parts:
            top = jnp.maximum(top, value if mask is None else jnp.where(mask, value, NEG))
        out = [jnp.exp(base - top)]
        for value, mask in parts:
            e = jnp.exp(value - top)
            out.append(e if mask is None else jnp.where(mask, e, 0.0))
        return top, out

    coefs += union(top_row, [(l_ab, None), (l_o, None), (l_c, None)])[1]
    tops = {}
    for name, table in (("c", ZC), ("b", ZB), ("o", PO)):
        masks = [by_head({k: table[k][i] for k in table}) for i in range(3)]
        tops[name], cs = union(top_row, list(zip((l_ab, l_o, l_c), masks)))
        coefs += cs
    coefs += union(tops["b"], [(l_a, by_head(PB_A))])[1]
    coefs += union(tops["b"], [(l_b, by_head(ZA_B))])[1]
    for i, cf in enumerate(coefs):
        ctab[i] = jnp.concatenate([cf] * (DV // 128), axis=1)

    carried = top_me + before
    prefix_top = carried[:, 0:1]
    b0 = rowst[0]
    cum = rowst[1]
    b = jnp.maximum(prefix_top, b0)
    rows_tmp[0:H, :] = jnp.exp(prefix_top - b) * (1.0 / 16.0)
    rows_tmp[H:2 * H, :] = jnp.exp(b0 - b) * (1.0 / 16.0)
    rows_tmp[2 * H:3 * H, :] = jnp.exp(-(cum + b))
    cols2[...] = rows_tmp[...].T
    fins_ref[H:2 * H, :] = top_all + total

    def normals():
        gathered(norms, snorm, rnorm)
        tot = jnp.zeros((H, DQK), F32)
        mine = jnp.zeros((H, DQK), F32)
        for i in range(NY * NZ):
            n = norms[i]
            w_all = jnp.exp(logs_ref(i) - top_all[:, 0:1])
            w_me = jnp.where(i < me, jnp.exp(logs_ref(i) - top_me[:, 0:1]), 0.0)
            tot = tot + w_all * n
            mine = mine + w_me * n
        pnorm[0:H, :] = mine
        turned = pltpu.roll(tot, lax.rem(DQK - me * (DQK // (NY * NZ)), DQK), 1)
        fins_ref[0:H, :] = turned[:, 0:128]

    def logs_ref(i):
        return logs[i][:, 0:1]

    def coef(i, h):
        return ctab[i, pl.ds(h, 1), :]

    STEP = 16

    def gather_b(u):
        h, c, rows = unit(u)
        na, nb, no, nc = path(h)

        @pl.when(z == nb)
        def _():
            remote(mem.at[h, rows], land1.at[h, rows], s0.at[u], r1.at[u], y, no).wait_recv()
            for t in range(ROWS // STEP):
                part = pl.ds(pl.multiple_of(c * ROWS + t * STEP, STEP), STEP)
                send1[h, part] = coef(0, h) * land1[h, part] + coef(1, h) * mem[h, part]
            remote(send1.at[h, rows], land1.at[h, rows], s0.at[u], r1.at[u], y, no).start()

    def own_o(u):
        h, c, rows = unit(u)
        na, nb, no, nc = path(h)

        @pl.when(z == no)
        def _():
            remote(mem.at[h, rows], land1.at[h, rows], s0.at[u], r1.at[u], y, nb).wait_recv()
            remote(mem.at[h, rows], land2.at[h, rows], s0.at[u], r2.at[u], y, nb).wait_recv()

            @pl.when(y == 0)
            def _():
                land3[h, rows] = jnp.zeros((ROWS, DV), F32)

            @pl.when(y > 0)
            def _():
                remote(mem.at[h, rows], land3.at[h, rows], s0.at[u], r3.at[u], y, nb).wait_recv()

            for t in range(ROWS // STEP):
                part = pl.ds(pl.multiple_of(c * ROWS + t * STEP, STEP), STEP)
                r = land3[h, part]
                xb = land1[h, part]
                xc = land2[h, part]
                mo = mem[h, part]

                def mix(i):
                    return coef(i, h) * r + coef(i + 1, h) * xb + coef(i + 2, h) * mo + coef(i + 3, h) * xc

                send1[h, part] = mix(2)
                land2[h, part] = mix(6)
                land1[h, part] = mix(10)
                pref[h, part] = mix(14).astype(BF16)

            @pl.when(y < NY - 1)
            def _():
                remote(send1.at[h, rows], land3.at[h, rows], s0.at[u], r3.at[u], y + 1, z).start()

            remote(land1.at[h, rows], land3.at[h, rows], s1.at[u], r3.at[u], y, nb).start()
            remote(land2.at[h, rows], land3.at[h, rows], s2.at[u], r3.at[u], y, nc).start()

            @pl.when(y == NY - 1)
            def _():
                for j in range(NZ):
                    part = pl.ds(pl.multiple_of(c * ROWS + j * STEP, STEP), STEP)

                    @pl.when((c != NY - 1) | (z != j))
                    def _():
                        remote(send1.at[h, part], fin.at[h], sf.at[u * NZ + j], rf.at[h], c, j).start()

                    @pl.when((c == NY - 1) & (z == j))
                    def _():
                        fin[h] = send1[h, part]

    def back_b(u):
        h, c, rows = unit(u)
        na, nb, no, nc = path(h)

        @pl.when(z == nb)
        def _():
            remote(mem.at[h, rows], land3.at[h, rows], s0.at[u], r3.at[u], y, no).wait_recv()
            for t in range(ROWS // STEP):
                part = pl.ds(pl.multiple_of(c * ROWS + t * STEP, STEP), STEP)
                zb = land3[h, part]
                pref[h, part] = (coef(18, h) * zb + coef(19, h) * land1[h, part]).astype(BF16)
                land3[h, part] = coef(20, h) * zb + coef(21, h) * mem[h, part]
            remote(land3.at[h, rows], land3.at[h, rows], s1.at[u], r3.at[u], y, na).start()

    def back_e(u):
        h, c, rows = unit(u)
        na, nb, no, nc = path(h)

        @pl.when((z == na) | (z == nc))
        def _():
            remote(mem.at[h, rows], land3.at[h, rows], s0.at[u], r3.at[u], y, nb).wait_recv()
            pref[h, rows] = land3[h, rows].astype(BF16)

    def sends_done(u, _):
        h, c, rows = unit(u)
        na, nb, no, nc = path(h)

        def done(sem):
            remote(mem.at[h, rows], land1.at[h, rows], sem, r1.at[u], y, nb).wait_send()

        @pl.when((z != no) | (y < NY - 1))
        def _():
            done(s0.at[u])

        @pl.when((z == nb) | (z == no))
        def _():
            done(s1.at[u])

        @pl.when(z == no)
        def _():
            done(s2.at[u])

        @pl.when((z == no) & (y == NY - 1))
        def _():
            for j in range(NZ):
                @pl.when((c != NY - 1) | (z != j))
                def _():
                    remote(
                        mem.at[h, pl.ds(0, STEP)], fin.at[h], sf.at[u * NZ + j], rf.at[h], y, nb
                    ).wait_send()
        return 0

    row_id = lax.broadcasted_iota(jnp.int32, (TILE, TILE), 0)
    col_id = lax.broadcasted_iota(jnp.int32, (TILE, TILE), 1)
    lane_id = lax.broadcasted_iota(jnp.int32, (TILE, 128), 1)

    def attend(h, i):
        q = qs[h, i * TILE:(i + 1) * TILE, :]
        bcol = column(cols1, i * TILE, TILE, h, H)
        total = jnp.zeros((TILE, DV), F32)
        den = jnp.zeros((TILE, 1), F32)
        for j in range(i + 1):
            span = slice(j * TILE, (j + 1) * TILE)
            s = lax.dot_general(q, ks[h, span, :], (((1,), (1,)), ((), ())), preferred_element_type=F32)
            p = jnp.exp(arow[pl.ds(h, 1), span] - bcol) * s
            if j == i:
                p = jnp.where(row_id >= col_id, p, 0.0)
            den = den + jnp.sum(p, axis=1, keepdims=True)
            total = total + jnp.dot(p.astype(BF16), vs[h, span, :], preferred_element_type=F32)
        acc[h, i * TILE:(i + 1) * TILE, :] = total
        at = slice(i * TILE, (i + 1) * TILE)
        dens[at, :] = jnp.where(lane_id == h, den, dens[at, :])

    def finish(h):
        def tile(i, _):
            at = pl.ds(pl.multiple_of(i * TILE, TILE), TILE)
            q = qs[h, at, :]
            carried_term = jnp.dot(q, pref[h], preferred_element_type=F32)
            qn = jnp.sum(q.astype(F32) * pnorm[pl.ds(h, 1), :], axis=1, keepdims=True)
            start = pl.multiple_of(i * TILE, TILE)
            w1 = column(cols2, start, TILE, h, 0)
            w2 = column(cols2, start, TILE, h, H)
            floor = column(cols2, start, TILE, h, 2 * H)
            den = column(dens, start, TILE, h, 0)
            bottom = jnp.maximum(jnp.abs(w1 * qn + w2 * den), floor)
            vs[h, at, :] = ((w1 * carried_term + w2 * acc[h, at, :]) / bottom).astype(BF16)
            return 0

        lax.fori_loop(0, LEN // TILE, tile, 0)

    lag_o = LAG_O + LAG_Y * y
    lag_b = lag_o + LAG_B
    lag_e = lag_b + LAG_E

    def guarded(fn, u):
        @pl.when((u >= 0) & (u < UNITS))
        def _():
            fn(jnp.clip(u, 0, UNITS - 1))

    def main(hh, _):
        @pl.when(hh + EARLY < H)
        def _():
            summarize(jnp.minimum(hh + EARLY, H - 1), 0)

        @pl.when(hh == H - EARLY)
        def _():
            spread(norms, snorm, rnorm)

        for c in range(PIECES):
            v = hh * PIECES + c
            guarded(first_send, v + LEAD)
            guarded(gather_b, v)
            guarded(own_o, v - lag_o)
            guarded(back_b, v - lag_b)
            guarded(back_e, v - lag_e)

            @pl.when((hh >= LAG_A) & (hh < H + LAG_A))
            def _():
                h = jnp.clip(hh - LAG_A, 0, H - 1)
                if c == 0:
                    pltpu.make_async_copy(q_hbm.at[:, 0:DQK], qs.at[h], in_sem.at[2 * H + h]).wait()
                attend(h, c)
        hf = hh - jnp.maximum((lag_e + PIECES - 1) // PIECES, max(H - EARLY + 1, LAG_A))

        @pl.when(hf == 0)
        def _():
            normals()

        @pl.when((hf >= 0) & (hf < H))
        def _():
            finish(jnp.clip(hf, 0, H - 1))
        return 0

    max_lag = LAG_O + LAG_Y * (NY - 1) + LAG_B + LAG_E
    lax.fori_loop(0, H + max((max_lag + PIECES - 1) // PIECES, H - EARLY + 1, LAG_A), main, 0)

    def last(h, _):
        na, nb, no, nc = path(h)

        @pl.when((y != NY - 1) | (z != no))
        def _():
            remote(mem.at[h, pl.ds(0, STEP)], fin.at[h], s0.at[0], rf.at[h], y, nb).wait_recv()
        finm_ref[h] = fin[h]
        return 0

    lax.fori_loop(0, H, last, 0)
    lax.fori_loop(0, UNITS, sends_done, 0)
    spread_done(stats, sstat, rstat)
    spread_done(norms, snorm, rnorm)


def write_out(heads, finm, fins, out_hbm, finm_hbm, norm_ref, stab_ref, sem):
    copies = [
        pltpu.make_async_copy(heads.at[h], out_hbm.at[:, h * DV:(h + 1) * DV], sem.at[h])
        for h in range(H)
    ]
    copies.append(pltpu.make_async_copy(finm, finm_hbm, sem.at[H]))
    for copy in copies:
        copy.start()
    norm_ref[...] = fins[0:H, 0:DQK // (NY * NZ)]
    stab_ref[...] = fins[H:2 * H, 0:1].reshape(H)
    for copy in copies:
        copy.wait()


def shards(query_matrix, key_vectors, value_vectors, input_gate, forget_gate):
    vmem = pl.BlockSpec(memory_space=pltpu.VMEM)
    hbm = pl.BlockSpec(memory_space=pl.ANY)
    dma = pltpu.SemaphoreType.DMA
    ctx = NY * NZ
    heads, final_memory, small = pl.pallas_call(
        kernel,
        out_shape=(
            pltpu.VMEM((H, LEN, DV), BF16),
            pltpu.VMEM((H, DQK // ctx, DV), F32),
            pltpu.VMEM((2 * H, 128), F32),
        ),
        in_specs=[hbm, hbm, hbm, vmem, vmem],
        out_specs=(vmem, vmem, vmem),
        scratch_shapes=[
            pltpu.VMEM((H, LEN, DQK), BF16),
            pltpu.VMEM((H, LEN, DQK), BF16),
            pltpu.VMEM((H, DQK, DV), F32),
            pltpu.VMEM((H, DQK, DV), F32),
            pltpu.VMEM((H, DQK, DV), F32),
            pltpu.VMEM((H, DQK, DV), F32),
            pltpu.VMEM((H, DQK, DV), F32),
            pltpu.VMEM((H, LEN, DV), F32),
            pltpu.VMEM((H, DQK, DV), BF16),
            pltpu.VMEM((LEN, 128), F32),
            pltpu.VMEM((LEN, 128), F32),
            pltpu.VMEM((LEN, 128), F32),
            pltpu.VMEM((128, LEN), F32),
            pltpu.VMEM((H, LEN), F32),
            pltpu.VMEM((2, H, LEN), F32),
            pltpu.VMEM((NCOEF, H, DV), F32),
            pltpu.VMEM((ctx, 2 * H, 128), F32),
            pltpu.VMEM((ctx, H, DQK), F32),
            pltpu.VMEM((H, DQK), F32),
            pltpu.VMEM((H, DQK // ctx, DV), F32),
            dma((3 * H,)),
            dma((UNITS,)),
            dma((UNITS,)),
            dma((UNITS,)),
            dma((UNITS,)),
            dma((UNITS,)),
            dma((UNITS,)),
            dma((UNITS * NZ,)),
            dma((H,)),
            dma((ctx,)),
            dma((ctx,)),
            dma((ctx,)),
            dma((ctx,)),
            dma((1,)),
        ],
        compiler_params=pltpu.CompilerParams(
            collective_id=0, has_side_effects=True, vmem_limit_bytes=57_000_000
        ),
        name="mlstm_cell",
    )(query_matrix, key_vectors, value_vectors, input_gate, forget_gate)
    return pl.pallas_call(
        write_out,
        out_shape=(
            jax.ShapeDtypeStruct((LEN, H * DV), BF16),
            jax.ShapeDtypeStruct((H, DQK // ctx, DV), F32),
            jax.ShapeDtypeStruct((H, DQK // ctx), F32),
            jax.ShapeDtypeStruct((H,), F32),
        ),
        in_specs=[hbm, hbm, vmem],
        out_specs=(hbm, hbm, vmem, vmem),
        scratch_shapes=[dma((H + 1,))],
        compiler_params=pltpu.CompilerParams(vmem_limit_bytes=1_000_000),
        name="write_out",
    )(heads, final_memory, small)


def solution(mesh):
    split = Mesh(mesh.devices.reshape(NY, NZ, mesh.shape["seq"]), ("ctx_0", "ctx_1", "seq"))
    return jax.shard_map(
        shards,
        mesh=split,
        in_specs=(
            P(SEQ_CTX, None),
            P(SEQ_CTX, None),
            P(SEQ_CTX, None),
            P(None, SEQ_CTX),
            P(None, SEQ_CTX),
        ),
        out_specs=(P(SEQ_CTX, None), P("seq", CTX, None), P("seq", CTX), P("seq")),
        check_vma=False,
    )
```

```python
import functools

import jax
import jax.numpy as jnp
from jax import lax
from jax.experimental import pallas as pl
from jax.experimental.pallas import tpu as pltpu
from jax.sharding import Mesh
from jax.sharding import PartitionSpec as P

H = 8
DQK = 256
DV = 512
LEN = 1024
NY = 4
NZ = 4
CTX = ("ctx_0", "ctx_1")
SEQ_CTX = ("seq", "ctx_0", "ctx_1")
NEG = -1e30
F32 = jnp.float32
BF16 = jnp.bfloat16
MESH = pl.DeviceIdType.MESH

PATHS = {
    1: (2, 1, 0, 3),
    2: (2, 3, 0, 1),
    3: (3, 2, 1, 0),
    4: (0, 1, 2, 3),
    5: (1, 2, 3, 0),
    6: (1, 0, 3, 2),
}
KINDS = (2, 5, 1, 3, 5, 4, 1, 6)
ZC = {1: (1, 1, 0), 2: (0, 1, 0), 3: (0, 0, 0), 4: (1, 1, 0), 5: (0, 0, 0), 6: (1, 0, 0)}
ZB = {1: (0, 1, 0), 2: (0, 1, 1), 3: (0, 1, 1), 4: (0, 0, 0), 5: (0, 0, 1), 6: (0, 0, 0)}
PO = {1: (0, 0, 0), 2: (0, 0, 0), 3: (0, 0, 1), 4: (1, 0, 0), 5: (1, 0, 1), 6: (1, 0, 1)}
PB_A = {1: 0, 2: 1, 3: 0, 4: 1, 5: 1, 6: 0}
ZA_B = {1: 1, 2: 0, 3: 1, 4: 0, 5: 0, 6: 1}

PIECES = 4
ROWS = DQK // PIECES
UNITS = H * PIECES
STEP = DQK // (NY * NZ)
SHARES = ROWS // STEP
TILES = 4
EACH = PIECES // TILES
LAG_O = 15
LAG_Y = 4
LAG_B = 12
LAG_E = 9
LAG_A = 1
LEAD = 17
EARLY = 8
NCOEF = 22
TILE = 256


def kernel(
    q_hbm, k_hbm, v_hbm, gate_hbm, forget_hbm,
    vs, finm_ref, fins_ref,
    qs, ks, mem, land1, land2, land3, send1, acc, pref,
    gate_ref, forget_ref, cols1, cols2, dens, rows_tmp, arow, rowst, ctab, stats, norms, pnorm, fin,
    in_sem, r1, r2, r3, s0, s1, s2, sf, rf, rstat, rnorm, sstat, snorm, gate_sem,
):
    y = lax.axis_index("ctx_0")
    z = lax.axis_index("ctx_1")
    me = y * NZ + z

    def remote(src, dst, ss, rs, yy, zz):
        return pltpu.make_async_remote_copy(
            src_ref=src, dst_ref=dst, send_sem=ss, recv_sem=rs,
            device_id={"ctx_0": yy, "ctx_1": zz}, device_id_type=MESH,
        )

    def load(hbm, dst, h, width, sem):
        return pltpu.make_async_copy(hbm.at[:, h * width:(h + 1) * width], dst.at[h], sem)

    barrier = pltpu.get_barrier_semaphore()

    def greet(i, _):
        peer = lax.rem(me + i, NY * NZ)
        pl.semaphore_signal(
            barrier, inc=1,
            device_id={"ctx_0": peer // NZ, "ctx_1": lax.rem(peer, NZ)}, device_id_type=MESH,
        )
        return 0

    gates = (
        pltpu.make_async_copy(gate_hbm, gate_ref, gate_sem.at[0]),
        pltpu.make_async_copy(forget_hbm, forget_ref, gate_sem.at[1]),
    )
    gates[1].start()
    gates[0].start()
    lax.fori_loop(1, NY * NZ, greet, 0)
    loads = []
    for h in range(H):
        loads.append((
            load(k_hbm, ks, h, DQK, in_sem.at[h]),
            load(v_hbm, vs, h, DV, in_sem.at[H + h]),
            load(q_hbm, qs, h, DQK, in_sem.at[2 * H + h]),
        ))
    for h in range(H):
        loads[h][0].start()
        loads[h][1].start()
    for h in range(H):
        loads[h][2].start()

    gates[0].wait()
    gates[1].wait()

    lane = lax.broadcasted_iota(jnp.int32, (H, LEN), 1)
    f = forget_ref[...]
    cum = jnp.minimum(f, 0.0) - jnp.log1p(jnp.exp(-jnp.abs(f)))
    for s in (1, 2, 4, 8, 16, 32, 64, 128, 256, 512):
        cum = cum + jnp.where(lane >= s, pltpu.roll(cum, s, 1), 0.0)
    a = gate_ref[...] - cum
    b0 = a
    for s in (1, 2, 4, 8, 16, 32, 64, 128, 256, 512):
        b0 = jnp.maximum(b0, jnp.where(lane >= s, pltpu.roll(b0, s, 1), NEG))
    arow[...] = a
    rowst[0] = b0
    rowst[1] = cum
    amax = b0[:, LEN - 1:LEN]
    rows_tmp[...] = jnp.zeros_like(rows_tmp)
    rows_tmp[0:H, :] = jnp.exp(a - amax)
    rows_tmp[H:2 * H, :] = b0
    cols1[...] = rows_tmp[...].T
    decay = cum[:, LEN - 1:LEN]
    stats[me, 0:H] = jnp.broadcast_to(decay + amax, (H, 128))
    stats[me, H:2 * H] = jnp.broadcast_to(decay, (H, 128))
    dens[...] = jnp.zeros_like(dens)

    pl.semaphore_wait(barrier, NY * NZ - 1)

    def spread(table, ss, rs):
        def one(i, _):
            peer = lax.rem(me + i, NY * NZ)
            remote(table.at[me], table.at[me], ss.at[peer], rs.at[me], peer // NZ, lax.rem(peer, NZ)).start()
            return 0
        lax.fori_loop(1, NY * NZ, one, 0)

    def gathered(table, ss, rs):
        def one(i, _):
            peer = lax.rem(me + i, NY * NZ)
            remote(table.at[peer], table.at[peer], ss.at[peer], rs.at[peer], y, z).wait_recv()
            return 0
        lax.fori_loop(1, NY * NZ, one, 0)

    def spread_done(table, ss, rs):
        def one(i, _):
            peer = lax.rem(me + i, NY * NZ)
            remote(table.at[me], table.at[me], ss.at[peer], rs.at[me], y, z).wait_send()
            return 0
        lax.fori_loop(1, NY * NZ, one, 0)

    spread(stats, sstat, rstat)

    roles = jnp.int32(0)
    for r in range(NZ):
        code = sum(PATHS[k].index(r) << (2 * h) for h, k in enumerate(KINDS))
        roles = jnp.where(z == r, jnp.int32(code), roles)
    steps = sum(((PATHS[k][1] - PATHS[k][0]) % NZ) << (2 * h) for h, k in enumerate(KINDS))

    def role(h):
        return jnp.right_shift(roles, 2 * h) & 3

    def along(h):
        return (z + (jnp.right_shift(jnp.int32(steps), 2 * h) & 3)) & 3

    def against(h):
        return (z + 4 - (jnp.right_shift(jnp.int32(steps), 2 * h) & 3)) & 3

    def unit(u):
        h = jnp.right_shift(u, PIECES.bit_length() - 1)
        c = u & (PIECES - 1)
        return h, c, pl.ds(pl.multiple_of(c * ROWS, ROWS), ROWS)

    def column(table, start, size, h, base):
        x = pltpu.roll(table[pl.ds(start, size), :], lax.rem(128 - h, 128), 1)
        return x[:, base:base + 1]

    def summarize(h, _):
        pltpu.make_async_copy(k_hbm.at[:, 0:DQK], ks.at[h], in_sem.at[h]).wait()
        pltpu.make_async_copy(v_hbm.at[:, 0:DV], vs.at[h], in_sem.at[H + h]).wait()
        scaled = ks[h].astype(F32) * column(cols1, 0, LEN, h, 0)
        norms[me, pl.ds(h, 1), :] = jnp.sum(scaled, axis=0, keepdims=True)
        mem[h] = lax.dot_general(
            scaled.astype(BF16), vs[h], (((0,), (0,)), ((), ())), preferred_element_type=F32
        )
        return 0

    def first_send(u):
        h, c, rows = unit(u)
        part = role(h)

        @pl.when(part == 0)
        def _():
            remote(mem.at[h, rows], land1.at[h, rows], s0.at[u], r1.at[u], y, along(h)).start()

        @pl.when(part == 3)
        def _():
            remote(mem.at[h, rows], land2.at[h, rows], s0.at[u], r2.at[u], y, against(h)).start()

    def begin(h, _):
        summarize(h, 0)
        for c in range(PIECES):
            @pl.when(h * PIECES + c < LEAD)
            def _():
                first_send(h * PIECES + c)
        return 0

    lax.fori_loop(0, EARLY, begin, 0)

    gathered(stats, sstat, rstat)
    sub = lax.broadcasted_iota(jnp.int32, (H, 128), 0)

    def by_head(table):
        out = jnp.zeros((H, 128), F32)
        for h in range(H):
            if table[KINDS[h]] != 0:
                out = jnp.where(sub == h, 1.0, out)
        return out > 0.5

    total = jnp.zeros((H, 128), F32)
    before = jnp.zeros((H, 128), F32)
    top_row = jnp.full((H, 128), NEG, F32)
    top_me = jnp.full((H, 128), NEG, F32)
    top_all = jnp.full((H, 128), NEG, F32)
    logs = []
    for i in range(NY * NZ):
        before = jnp.where(me == i, total, before)
        dec = stats[i, H:2 * H]
        total = total + dec
        w = stats[i, 0:H] - total
        logs.append(w)
        top_row = jnp.maximum(top_row, jnp.where(i < y * NZ, w, NEG))
        top_me = jnp.maximum(top_me, jnp.where(i < me, w, NEG))
        top_all = jnp.maximum(top_all, w)
    here = []
    for j in range(NZ):
        w = logs[j]
        for r in range(1, NY):
            w = jnp.where(y == r, logs[r * NZ + j], w)
        here.append(w)

    def node(i):
        out = here[0]
        for j in range(1, NZ):
            mask = by_head({k: int(PATHS[k][i] == j) for k in PATHS})
            out = jnp.where(mask, here[j], out)
        return out

    l_a, l_b, l_o, l_c = (node(i) for i in range(4))
    l_ab = jnp.maximum(l_a, l_b)
    coefs = [jnp.exp(l_a - l_ab), jnp.exp(l_b - l_ab)]

    def union(base, parts):
        top = base
        for value, mask in parts:
            top = jnp.maximum(top, value if mask is None else jnp.where(mask, value, NEG))
        out = [jnp.exp(base - top)]
        for value, mask in parts:
            e = jnp.exp(value - top)
            out.append(e if mask is None else jnp.where(mask, e, 0.0))
        return top, out

    coefs += union(top_row, [(l_ab, None), (l_o, None), (l_c, None)])[1]
    tops = {}
    for name, table in (("c", ZC), ("b", ZB), ("o", PO)):
        masks = [by_head({k: table[k][i] for k in table}) for i in range(3)]
        tops[name], cs = union(top_row, list(zip((l_ab, l_o, l_c), masks)))
        coefs += cs
    coefs += union(tops["b"], [(l_a, by_head(PB_A))])[1]
    coefs += union(tops["b"], [(l_b, by_head(ZA_B))])[1]
    for i, cf in enumerate(coefs):
        ctab[i] = jnp.concatenate([cf] * (DV // 128), axis=1)

    carried = top_me + before
    prefix_top = carried[:, 0:1]
    b0 = rowst[0]
    cum = rowst[1]
    b = jnp.maximum(prefix_top, b0)
    rows_tmp[0:H, :] = jnp.exp(prefix_top - b) * (1.0 / 16.0)
    rows_tmp[H:2 * H, :] = jnp.exp(b0 - b) * (1.0 / 16.0)
    rows_tmp[2 * H:3 * H, :] = jnp.exp(-(cum + b))
    cols2[...] = rows_tmp[...].T
    fins_ref[H:2 * H, :] = top_all + total

    def normals():
        gathered(norms, snorm, rnorm)
        tot = jnp.zeros((H, DQK), F32)
        mine = jnp.zeros((H, DQK), F32)
        for i in range(NY * NZ):
            n = norms[i]
            w_all = jnp.exp(logs_ref(i) - top_all[:, 0:1])
            w_me = jnp.where(i < me, jnp.exp(logs_ref(i) - top_me[:, 0:1]), 0.0)
            tot = tot + w_all * n
            mine = mine + w_me * n
        pnorm[0:H, :] = mine
        turned = pltpu.roll(tot, lax.rem(DQK - me * (DQK // (NY * NZ)), DQK), 1)
        fins_ref[0:H, :] = turned[:, 0:128]

    def logs_ref(i):
        return logs[i][:, 0:1]

    def coef(i, h):
        return ctab[i, pl.ds(h, 1), :]

    def gather_b(u):
        h, c, rows = unit(u)
        @pl.when(role(h) == 1)
        def _():
            remote(mem.at[h, rows], land1.at[h, rows], s0.at[u], r1.at[u], y, along(h)).wait_recv()
            for t in range(ROWS // STEP):
                part = pl.ds(pl.multiple_of(c * ROWS + t * STEP, STEP), STEP)
                send1[h, part] = coef(0, h) * land1[h, part] + coef(1, h) * mem[h, part]
            remote(send1.at[h, rows], land1.at[h, rows], s0.at[u], r1.at[u], y, along(h)).start()

    def own_o(u):
        h, c, rows = unit(u)
        @pl.when(role(h) == 2)
        def _():
            remote(mem.at[h, rows], land1.at[h, rows], s0.at[u], r1.at[u], y, along(h)).wait_recv()
            remote(mem.at[h, rows], land2.at[h, rows], s0.at[u], r2.at[u], y, along(h)).wait_recv()

            @pl.when(y == 0)
            def _():
                land3[h, rows] = jnp.zeros((ROWS, DV), F32)

            @pl.when(y > 0)
            def _():
                remote(mem.at[h, rows], land3.at[h, rows], s0.at[u], r3.at[u], y, along(h)).wait_recv()

            for t in range(ROWS // STEP):
                part = pl.ds(pl.multiple_of(c * ROWS + t * STEP, STEP), STEP)
                r = land3[h, part]
                xb = land1[h, part]
                xc = land2[h, part]
                mo = mem[h, part]

                def mix(i):
                    return coef(i, h) * r + coef(i + 1, h) * xb + coef(i + 2, h) * mo + coef(i + 3, h) * xc

                send1[h, part] = mix(2)
                land2[h, part] = mix(6)
                land1[h, part] = mix(10)
                pref[h, part] = mix(14).astype(BF16)

            @pl.when(y < NY - 1)
            def _():
                remote(send1.at[h, rows], land3.at[h, rows], s0.at[u], r3.at[u], y + 1, z).start()

            remote(land1.at[h, rows], land3.at[h, rows], s1.at[u], r3.at[u], y, against(h)).start()
            remote(land2.at[h, rows], land3.at[h, rows], s2.at[u], r3.at[u], y, along(h)).start()

            @pl.when(y == NY - 1)
            def _():
                for j in range(SHARES):
                    part = pl.ds(pl.multiple_of(c * ROWS + j * STEP, STEP), STEP)
                    to = c * SHARES + j

                    @pl.when(to != me)
                    def _():
                        remote(
                            send1.at[h, part], fin.at[h], sf.at[u * SHARES + j], rf.at[h],
                            jnp.right_shift(to, 2), to & 3,
                        ).start()

                    @pl.when(to == me)
                    def _():
                        fin[h] = send1[h, part]

    def back_b(u):
        h, c, rows = unit(u)
        @pl.when(role(h) == 1)
        def _():
            remote(mem.at[h, rows], land3.at[h, rows], s0.at[u], r3.at[u], y, along(h)).wait_recv()
            for t in range(ROWS // STEP):
                part = pl.ds(pl.multiple_of(c * ROWS + t * STEP, STEP), STEP)
                zb = land3[h, part]
                pref[h, part] = (coef(18, h) * zb + coef(19, h) * land1[h, part]).astype(BF16)
                land3[h, part] = coef(20, h) * zb + coef(21, h) * mem[h, part]
            remote(land3.at[h, rows], land3.at[h, rows], s1.at[u], r3.at[u], y, against(h)).start()

    def back_e(u):
        h, c, rows = unit(u)
        @pl.when((role(h) == 0) | (role(h) == 3))
        def _():
            remote(mem.at[h, rows], land3.at[h, rows], s0.at[u], r3.at[u], y, along(h)).wait_recv()
            pref[h, rows] = land3[h, rows].astype(BF16)

    def sends_done(h, _):
        part = role(h)
        small = pl.ds(0, STEP)

        def done(sem):
            for c in range(PIECES):
                rows = pl.ds(c * ROWS, ROWS)
                remote(mem.at[h, rows], land1.at[h, rows], sem.at[h * PIECES + c], r1.at[0], y, along(h)).wait_send()

        @pl.when((part != 2) | (y < NY - 1))
        def _():
            done(s0)

        @pl.when((part == 1) | (part == 2))
        def _():
            done(s1)

        @pl.when(part == 2)
        def _():
            done(s2)

        @pl.when((part == 2) & (y == NY - 1))
        def _():
            for i in range(NY * NZ):
                def one():
                    remote(
                        mem.at[h, small], fin.at[h], sf.at[h * NY * NZ + i], rf.at[h], y, along(h)
                    ).wait_send()

                if i < (NY - 1) * NZ:
                    one()
                else:
                    pl.when(z != i - (NY - 1) * NZ)(one)
        return 0

    row_id = lax.broadcasted_iota(jnp.int32, (TILE, TILE), 0)
    col_id = lax.broadcasted_iota(jnp.int32, (TILE, TILE), 1)
    lane_id = lax.broadcasted_iota(jnp.int32, (TILE, 128), 1)

    def attend(h, i):
        q = qs[h, i * TILE:(i + 1) * TILE, :]
        bcol = column(cols1, i * TILE, TILE, h, H)
        total = jnp.zeros((TILE, DV), F32)
        den = jnp.zeros((TILE, 1), F32)
        for j in range(i + 1):
            span = slice(j * TILE, (j + 1) * TILE)
            s = lax.dot_general(q, ks[h, span, :], (((1,), (1,)), ((), ())), preferred_element_type=F32)
            p = jnp.exp(arow[pl.ds(h, 1), span] - bcol) * s
            if j == i:
                p = jnp.where(row_id >= col_id, p, 0.0)
            den = den + jnp.sum(p, axis=1, keepdims=True)
            total = total + jnp.dot(p.astype(BF16), vs[h, span, :], preferred_element_type=F32)
        w2 = column(cols2, i * TILE, TILE, h, H)
        acc[h, i * TILE:(i + 1) * TILE, :] = w2 * total
        at = slice(i * TILE, (i + 1) * TILE)
        dens[at, :] = jnp.where(lane_id == h, w2 * den, dens[at, :])

    def finish(h, i):
        at = slice(i * TILE, (i + 1) * TILE)
        q = qs[h, at, :]
        qn = jnp.sum(q.astype(F32) * pnorm[pl.ds(h, 1), :], axis=1, keepdims=True)
        w1 = column(cols2, i * TILE, TILE, h, 0)
        floor = column(cols2, i * TILE, TILE, h, 2 * H)
        den = column(dens, i * TILE, TILE, h, 0)
        inverse = 1.0 / jnp.maximum(jnp.abs(w1 * qn + den), floor)
        carried_term = jnp.dot(q, pref[h], preferred_element_type=F32)
        vs[h, at, :] = ((w1 * carried_term + acc[h, at, :]) * inverse).astype(BF16)

    lag_o = LAG_O + LAG_Y * y
    lag_b = lag_o + LAG_B
    lag_e = lag_b + LAG_E

    def guarded(fn, u):
        @pl.when((u >= 0) & (u < UNITS))
        def _():
            fn(jnp.clip(u, 0, UNITS - 1))

    lag_f = jnp.maximum(jnp.right_shift(lag_e + PIECES - 1, PIECES.bit_length() - 1), max(H - EARLY + 1, LAG_A)) + 1

    def main(hh, _):
        @pl.when(hh + EARLY < H)
        def _():
            summarize(jnp.minimum(hh + EARLY, H - 1), 0)

        @pl.when(hh == H - EARLY)
        def _():
            spread(norms, snorm, rnorm)

        hf = hh - lag_f

        @pl.when(hf == 0)
        def _():
            normals()

        for c in range(PIECES):
            v = hh * PIECES + c
            guarded(first_send, v + LEAD)
            guarded(gather_b, v)
            guarded(own_o, v - lag_o)
            guarded(back_b, v - lag_b)
            guarded(back_e, v - lag_e)

            if c % EACH == 0:
                @pl.when((hh >= LAG_A) & (hh < H + LAG_A))
                def _():
                    h = jnp.clip(hh - LAG_A, 0, H - 1)
                    if c == 0:
                        pltpu.make_async_copy(q_hbm.at[:, 0:DQK], qs.at[h], in_sem.at[2 * H + h]).wait()
                    attend(h, c // EACH)

            if c % EACH == EACH // 2:
                @pl.when((hf >= 0) & (hf < H))
                def _():
                    finish(jnp.clip(hf, 0, H - 1), c // EACH)
        return 0

    max_lag = LAG_O + LAG_Y * (NY - 1) + LAG_B + LAG_E
    lax.fori_loop(0, H + max((max_lag + PIECES - 1) // PIECES, H - EARLY + 1, LAG_A) + 1, main, 0)

    def last(h, _):
        @pl.when((y != NY - 1) | (role(h) != 2))
        def _():
            remote(mem.at[h, pl.ds(0, STEP)], fin.at[h], s0.at[0], rf.at[h], y, along(h)).wait_recv()
        finm_ref[h] = fin[h]
        return 0

    lax.fori_loop(0, H, last, 0)
    lax.fori_loop(0, H, sends_done, 0)
    spread_done(stats, sstat, rstat)
    spread_done(norms, snorm, rnorm)


def write_out(heads, finm, fins, out_hbm, finm_hbm, norm_ref, stab_ref, sem):
    copies = [
        pltpu.make_async_copy(heads.at[h], out_hbm.at[:, h * DV:(h + 1) * DV], sem.at[h])
        for h in range(H)
    ]
    copies.append(pltpu.make_async_copy(finm, finm_hbm, sem.at[H]))
    for copy in copies:
        copy.start()
    norm_ref[...] = fins[0:H, 0:DQK // (NY * NZ)]
    stab_ref[...] = fins[H:2 * H, 0:1].reshape(H)
    for copy in copies:
        copy.wait()


def shards(query_matrix, key_vectors, value_vectors, input_gate, forget_gate):
    vmem = pl.BlockSpec(memory_space=pltpu.VMEM)
    hbm = pl.BlockSpec(memory_space=pl.ANY)
    dma = pltpu.SemaphoreType.DMA
    ctx = NY * NZ
    heads, final_memory, small = pl.pallas_call(
        kernel,
        out_shape=(
            pltpu.VMEM((H, LEN, DV), BF16),
            pltpu.VMEM((H, DQK // ctx, DV), F32),
            pltpu.VMEM((2 * H, 128), F32),
        ),
        in_specs=[hbm] * 5,
        out_specs=(vmem, vmem, vmem),
        scratch_shapes=[
            pltpu.VMEM((H, LEN, DQK), BF16),
            pltpu.VMEM((H, LEN, DQK), BF16),
            pltpu.VMEM((H, DQK, DV), F32),
            pltpu.VMEM((H, DQK, DV), F32),
            pltpu.VMEM((H, DQK, DV), F32),
            pltpu.VMEM((H, DQK, DV), F32),
            pltpu.VMEM((H, DQK, DV), F32),
            pltpu.VMEM((H, LEN, DV), F32),
            pltpu.VMEM((H, DQK, DV), BF16),
            pltpu.VMEM((H, LEN), F32),
            pltpu.VMEM((H, LEN), F32),
            pltpu.VMEM((LEN, 128), F32),
            pltpu.VMEM((LEN, 128), F32),
            pltpu.VMEM((LEN, 128), F32),
            pltpu.VMEM((128, LEN), F32),
            pltpu.VMEM((H, LEN), F32),
            pltpu.VMEM((2, H, LEN), F32),
            pltpu.VMEM((NCOEF, H, DV), F32),
            pltpu.VMEM((ctx, 2 * H, 128), F32),
            pltpu.VMEM((ctx, H, DQK), F32),
            pltpu.VMEM((H, DQK), F32),
            pltpu.VMEM((H, DQK // ctx, DV), F32),
            dma((3 * H,)),
            dma((UNITS,)),
            dma((UNITS,)),
            dma((UNITS,)),
            dma((UNITS,)),
            dma((UNITS,)),
            dma((UNITS,)),
            dma((UNITS * SHARES,)),
            dma((H,)),
            dma((ctx,)),
            dma((ctx,)),
            dma((ctx,)),
            dma((ctx,)),
            dma((2,)),
        ],
        compiler_params=pltpu.CompilerParams(
            collective_id=0, has_side_effects=True, vmem_limit_bytes=57_000_000
        ),
        name="mlstm_cell",
    )(query_matrix, key_vectors, value_vectors, input_gate, forget_gate)
    return pl.pallas_call(
        write_out,
        out_shape=(
            jax.ShapeDtypeStruct((LEN, H * DV), BF16),
            jax.ShapeDtypeStruct((H, DQK // ctx, DV), F32),
            jax.ShapeDtypeStruct((H, DQK // ctx), F32),
            jax.ShapeDtypeStruct((H,), F32),
        ),
        in_specs=[hbm, hbm, vmem],
        out_specs=(hbm, hbm, vmem, vmem),
        scratch_shapes=[dma((H + 1,))],
        compiler_params=pltpu.CompilerParams(vmem_limit_bytes=1_000_000),
        name="write_out",
    )(heads, final_memory, small)


def solution(mesh):
    split = Mesh(mesh.devices.reshape(NY, NZ, mesh.shape["seq"]), ("ctx_0", "ctx_1", "seq"))
    return jax.shard_map(
        shards,
        mesh=split,
        in_specs=(
            P(SEQ_CTX, None),
            P(SEQ_CTX, None),
            P(SEQ_CTX, None),
            P(None, SEQ_CTX),
            P(None, SEQ_CTX),
        ),
        out_specs=(P(SEQ_CTX, None), P("seq", CTX, None), P("seq", CTX), P("seq")),
        check_vma=False,
    )
```

```python
import functools

import jax
import jax.numpy as jnp
from jax import lax
from jax.experimental import pallas as pl
from jax.experimental.pallas import tpu as pltpu
from jax.sharding import Mesh
from jax.sharding import PartitionSpec as P

H = 8
DQK = 256
DV = 512
LEN = 1024
NY = 4
NZ = 4
CTX = ("ctx_0", "ctx_1")
SEQ_CTX = ("seq", "ctx_0", "ctx_1")
NEG = -1e30
F32 = jnp.float32
BF16 = jnp.bfloat16
MESH = pl.DeviceIdType.MESH

PATHS = {
    1: (2, 1, 0, 3),
    2: (2, 3, 0, 1),
    3: (3, 2, 1, 0),
    4: (0, 1, 2, 3),
    5: (1, 2, 3, 0),
    6: (1, 0, 3, 2),
}
KINDS = (1, 2, 5, 2, 4, 3, 5, 1, 1, 3, 5, 4, 1, 4, 6, 6)
ZC = {1: (1, 1, 0), 2: (0, 1, 0), 3: (0, 0, 0), 4: (1, 1, 0), 5: (0, 0, 0), 6: (1, 0, 0)}
ZB = {1: (0, 1, 0), 2: (0, 1, 1), 3: (0, 1, 1), 4: (0, 0, 0), 5: (0, 0, 1), 6: (0, 0, 0)}
PO = {1: (0, 0, 0), 2: (0, 0, 0), 3: (0, 0, 1), 4: (1, 0, 0), 5: (1, 0, 1), 6: (1, 0, 1)}
PB_A = {1: 0, 2: 1, 3: 0, 4: 1, 5: 1, 6: 0}
ZA_B = {1: 1, 2: 0, 3: 1, 4: 0, 5: 0, 6: 1}

PIECES = 4
ROWS = DQK // PIECES
UNITS = H * PIECES
STEP = DQK // (NY * NZ)
SHARES = ROWS // STEP
TILES = 4
EACH = PIECES // TILES
LAG_O = 15
LAG_Y = 1
LAG_B = 17
LAG_E = 17
LAG_A = 0
LEAD = 15
EARLY = 8
NCOEF = 22
TILE = 256


def kernel(
    q_hbm, k_hbm, v_hbm, gate_hbm, forget_hbm,
    vs, finm_ref, fins_ref,
    qs, ks, mem, land1, land2, land3, send1, acc, pref,
    gate_ref, forget_ref, cols1, cols2, dens, rows_tmp, arow, rowst, ctab, stats, norms, pnorm, fin,
    in_sem, r1, r2, r3, s0, s1, s2, sf, rf, rstat, rnorm, sstat, snorm, gate_sem,
):
    y = lax.axis_index("ctx_0")
    z = lax.axis_index("ctx_1")
    me = y * NZ + z

    def remote(src, dst, ss, rs, yy, zz):
        return pltpu.make_async_remote_copy(
            src_ref=src, dst_ref=dst, send_sem=ss, recv_sem=rs,
            device_id={"ctx_0": yy, "ctx_1": zz}, device_id_type=MESH,
        )

    def load(hbm, dst, h, width, sem):
        return pltpu.make_async_copy(hbm.at[:, h * width:(h + 1) * width], dst.at[h], sem)

    barrier = pltpu.get_barrier_semaphore()

    def greet(i, _):
        peer = lax.rem(me + i, NY * NZ)
        pl.semaphore_signal(
            barrier, inc=1,
            device_id={"ctx_0": peer // NZ, "ctx_1": lax.rem(peer, NZ)}, device_id_type=MESH,
        )
        return 0

    gates = (
        pltpu.make_async_copy(gate_hbm, gate_ref, gate_sem.at[0]),
        pltpu.make_async_copy(forget_hbm, forget_ref, gate_sem.at[1]),
    )
    gates[1].start()
    gates[0].start()
    lax.fori_loop(1, NY * NZ, greet, 0)
    loads = []
    for h in range(H):
        loads.append((
            load(k_hbm, ks, h, DQK, in_sem.at[h]),
            load(v_hbm, vs, h, DV, in_sem.at[H + h]),
            load(q_hbm, qs, h, DQK, in_sem.at[2 * H + h]),
        ))
    for h in range(H):
        loads[h][0].start()
        loads[h][1].start()
    for h in range(H):
        loads[h][2].start()

    gates[0].wait()
    gates[1].wait()

    lane = lax.broadcasted_iota(jnp.int32, (H, LEN), 1)
    f = forget_ref[...]
    cum = jnp.minimum(f, 0.0) - jnp.log1p(jnp.exp(-jnp.abs(f)))
    for s in (1, 2, 4, 8, 16, 32, 64, 128, 256, 512):
        cum = cum + jnp.where(lane >= s, pltpu.roll(cum, s, 1), 0.0)
    a = gate_ref[...] - cum
    b0 = a
    for s in (1, 2, 4, 8, 16, 32, 64, 128, 256, 512):
        b0 = jnp.maximum(b0, jnp.where(lane >= s, pltpu.roll(b0, s, 1), NEG))
    arow[...] = a
    rowst[0] = b0
    rowst[1] = cum
    amax = b0[:, LEN - 1:LEN]
    rows_tmp[...] = jnp.zeros_like(rows_tmp)
    rows_tmp[0:H, :] = jnp.exp(a - amax)
    rows_tmp[H:2 * H, :] = b0
    cols1[...] = rows_tmp[...].T
    decay = cum[:, LEN - 1:LEN]
    stats[me, 0:H] = jnp.broadcast_to(decay + amax, (H, 128))
    stats[me, H:2 * H] = jnp.broadcast_to(decay, (H, 128))
    dens[...] = jnp.zeros_like(dens)

    pl.semaphore_wait(barrier, NY * NZ - 1)

    def spread(table, ss, rs):
        def one(i, _):
            peer = lax.rem(me + i, NY * NZ)
            remote(table.at[me], table.at[me], ss.at[peer], rs.at[me], peer // NZ, lax.rem(peer, NZ)).start()
            return 0
        lax.fori_loop(1, NY * NZ, one, 0)

    def gathered(table, ss, rs):
        def one(i, _):
            peer = lax.rem(me + i, NY * NZ)
            remote(table.at[peer], table.at[peer], ss.at[peer], rs.at[peer], y, z).wait_recv()
            return 0
        lax.fori_loop(1, NY * NZ, one, 0)

    def spread_done(table, ss, rs):
        def one(i, _):
            peer = lax.rem(me + i, NY * NZ)
            remote(table.at[me], table.at[me], ss.at[peer], rs.at[me], y, z).wait_send()
            return 0
        lax.fori_loop(1, NY * NZ, one, 0)

    spread(stats, sstat, rstat)

    roles = []
    steps = []
    for first in (0, H):
        mine = jnp.int32(0)
        kinds = KINDS[first:first + H]
        for r in range(NZ):
            code = sum(PATHS[k].index(r) << (2 * i) for i, k in enumerate(kinds))
            mine = jnp.where(z == r, jnp.int32(code), mine)
        roles.append(mine)
        steps.append(sum(((PATHS[k][1] - PATHS[k][0]) % NZ) << (2 * i) for i, k in enumerate(kinds)))

    def digit(pair, g):
        word = jnp.where(g < H, jnp.int32(pair[0]), jnp.int32(pair[1]))
        return jnp.right_shift(word, 2 * (g & (H - 1))) & 3

    def role(g):
        return digit(roles, g)

    def along(g):
        return (z + digit(steps, g)) & 3

    def against(g):
        return (z + 4 - digit(steps, g)) & 3

    def unit(u):
        h = jnp.right_shift(u, PIECES.bit_length() - 1)
        c = u & (PIECES - 1)
        return h, jnp.right_shift(u, PIECES.bit_length() - 2), c, pl.ds(pl.multiple_of(c * ROWS, ROWS), ROWS)

    def column(table, start, size, h, base):
        x = pltpu.roll(table[pl.ds(start, size), :], lax.rem(128 - h, 128), 1)
        return x[:, base:base + 1]

    def summarize(h, _):
        pltpu.make_async_copy(k_hbm.at[:, 0:DQK], ks.at[h], in_sem.at[h]).wait()
        pltpu.make_async_copy(v_hbm.at[:, 0:DV], vs.at[h], in_sem.at[H + h]).wait()
        scaled = ks[h].astype(F32) * column(cols1, 0, LEN, h, 0)
        norms[me, pl.ds(h, 1), :] = jnp.sum(scaled, axis=0, keepdims=True)
        mem[h] = lax.dot_general(
            scaled.astype(BF16), vs[h], (((0,), (0,)), ((), ())), preferred_element_type=F32
        )
        return 0

    def first_send(u):
        h, g, c, rows = unit(u)
        part = role(g)

        @pl.when(part == 0)
        def _():
            remote(mem.at[h, rows], land1.at[h, rows], s0.at[u], r1.at[u], y, along(g)).start()

        @pl.when(part == 3)
        def _():
            remote(mem.at[h, rows], land2.at[h, rows], s0.at[u], r2.at[u], y, against(g)).start()

    def begin(h, _):
        summarize(h, 0)
        for c in range(PIECES):
            @pl.when(h * PIECES + c < LEAD)
            def _():
                first_send(h * PIECES + c)
        return 0

    lax.fori_loop(0, EARLY, begin, 0)

    gathered(stats, sstat, rstat)
    sub = lax.broadcasted_iota(jnp.int32, (H, 128), 0)

    total = jnp.zeros((H, 128), F32)
    before = jnp.zeros((H, 128), F32)
    top_row = jnp.full((H, 128), NEG, F32)
    top_me = jnp.full((H, 128), NEG, F32)
    top_all = jnp.full((H, 128), NEG, F32)
    logs = []
    for i in range(NY * NZ):
        before = jnp.where(me == i, total, before)
        dec = stats[i, H:2 * H]
        total = total + dec
        w = stats[i, 0:H] - total
        logs.append(w)
        top_row = jnp.maximum(top_row, jnp.where(i < y * NZ, w, NEG))
        top_me = jnp.maximum(top_me, jnp.where(i < me, w, NEG))
        top_all = jnp.maximum(top_all, w)
    here = []
    for j in range(NZ):
        w = logs[j]
        for r in range(1, NY):
            w = jnp.where(y == r, logs[r * NZ + j], w)
        here.append(w)

    def by_head(half, table):
        out = jnp.zeros((H, 128), F32)
        for h in range(H):
            if table[KINDS[2 * h + half]] != 0:
                out = jnp.where(sub == h, 1.0, out)
        return out > 0.5

    def union(base, parts):
        top = base
        for value, mask in parts:
            top = jnp.maximum(top, value if mask is None else jnp.where(mask, value, NEG))
        out = [jnp.exp(base - top)]
        for value, mask in parts:
            e = jnp.exp(value - top)
            out.append(e if mask is None else jnp.where(mask, e, 0.0))
        return top, out

    for half in range(2):
        def node(i):
            out = here[0]
            for j in range(1, NZ):
                out = jnp.where(by_head(half, {k: int(PATHS[k][i] == j) for k in PATHS}), here[j], out)
            return out

        l_a, l_b, l_o, l_c = (node(i) for i in range(4))
        l_ab = jnp.maximum(l_a, l_b)
        coefs = [jnp.exp(l_a - l_ab), jnp.exp(l_b - l_ab)]
        coefs += union(top_row, [(l_ab, None), (l_o, None), (l_c, None)])[1]
        tops = {}
        for name, table in (("c", ZC), ("b", ZB), ("o", PO)):
            masks = [by_head(half, {k: table[k][i] for k in table}) for i in range(3)]
            tops[name], cs = union(top_row, list(zip((l_ab, l_o, l_c), masks)))
            coefs += cs
        coefs += union(tops["b"], [(l_a, by_head(half, PB_A))])[1]
        coefs += union(tops["b"], [(l_b, by_head(half, ZA_B))])[1]
        for i, cf in enumerate(coefs):
            ctab[half, i] = jnp.concatenate([cf] * (DV // 128), axis=1)

    carried = top_me + before
    prefix_top = carried[:, 0:1]
    b0 = rowst[0]
    cum = rowst[1]
    b = jnp.maximum(prefix_top, b0)
    rows_tmp[0:H, :] = jnp.exp(prefix_top - b) * (1.0 / 16.0)
    rows_tmp[H:2 * H, :] = jnp.exp(b0 - b) * (1.0 / 16.0)
    rows_tmp[2 * H:3 * H, :] = jnp.exp(-(cum + b))
    cols2[...] = rows_tmp[...].T
    fins_ref[H:2 * H, :] = top_all + total

    def normals():
        gathered(norms, snorm, rnorm)
        tot = jnp.zeros((H, DQK), F32)
        mine = jnp.zeros((H, DQK), F32)
        for i in range(NY * NZ):
            n = norms[i]
            w_all = jnp.exp(logs_ref(i) - top_all[:, 0:1])
            w_me = jnp.where(i < me, jnp.exp(logs_ref(i) - top_me[:, 0:1]), 0.0)
            tot = tot + w_all * n
            mine = mine + w_me * n
        pnorm[0:H, :] = mine
        turned = pltpu.roll(tot, lax.rem(DQK - me * (DQK // (NY * NZ)), DQK), 1)
        fins_ref[0:H, :] = turned[:, 0:128]

    def logs_ref(i):
        return logs[i][:, 0:1]

    def coef(i, h, g):
        return ctab[g & 1, i, pl.ds(h, 1), :]

    def gather_b(u):
        h, g, c, rows = unit(u)
        @pl.when(role(g) == 1)
        def _():
            remote(mem.at[h, rows], land1.at[h, rows], s0.at[u], r1.at[u], y, along(g)).wait_recv()
            for t in range(ROWS // STEP):
                part = pl.ds(pl.multiple_of(c * ROWS + t * STEP, STEP), STEP)
                send1[h, part] = coef(0, h, g) * land1[h, part] + coef(1, h, g) * mem[h, part]
            remote(send1.at[h, rows], land1.at[h, rows], s0.at[u], r1.at[u], y, along(g)).start()

    def own_o(u):
        h, g, c, rows = unit(u)
        @pl.when(role(g) == 2)
        def _():
            remote(mem.at[h, rows], land1.at[h, rows], s0.at[u], r1.at[u], y, along(g)).wait_recv()
            remote(mem.at[h, rows], land2.at[h, rows], s0.at[u], r2.at[u], y, along(g)).wait_recv()

            @pl.when(y == 0)
            def _():
                land3[h, rows] = jnp.zeros((ROWS, DV), F32)

            @pl.when(y > 0)
            def _():
                remote(mem.at[h, rows], land3.at[h, rows], s0.at[u], r3.at[u], y, along(g)).wait_recv()

            for t in range(ROWS // STEP):
                part = pl.ds(pl.multiple_of(c * ROWS + t * STEP, STEP), STEP)
                r = land3[h, part]
                xb = land1[h, part]
                xc = land2[h, part]
                mo = mem[h, part]

                def mix(i):
                    return coef(i, h, g) * r + coef(i + 1, h, g) * xb + coef(i + 2, h, g) * mo + coef(i + 3, h, g) * xc

                send1[h, part] = mix(2)
                land2[h, part] = mix(6)
                land1[h, part] = mix(10)
                pref[h, part] = mix(14).astype(BF16)

            @pl.when(y < NY - 1)
            def _():
                remote(send1.at[h, rows], land3.at[h, rows], s0.at[u], r3.at[u], y + 1, z).start()

            remote(land1.at[h, rows], land3.at[h, rows], s1.at[u], r3.at[u], y, against(g)).start()
            remote(land2.at[h, rows], land3.at[h, rows], s2.at[u], r3.at[u], y, along(g)).start()

            @pl.when(y == NY - 1)
            def _():
                for j in range(SHARES):
                    part = pl.ds(pl.multiple_of(c * ROWS + j * STEP, STEP), STEP)
                    to = c * SHARES + j

                    @pl.when(to != me)
                    def _():
                        remote(
                            send1.at[h, part], fin.at[h], sf.at[u * SHARES + j], rf.at[h],
                            jnp.right_shift(to, 2), to & 3,
                        ).start()

                    @pl.when(to == me)
                    def _():
                        fin[h] = send1[h, part]

    def back_b(u):
        h, g, c, rows = unit(u)
        @pl.when(role(g) == 1)
        def _():
            remote(mem.at[h, rows], land3.at[h, rows], s0.at[u], r3.at[u], y, along(g)).wait_recv()
            for t in range(ROWS // STEP):
                part = pl.ds(pl.multiple_of(c * ROWS + t * STEP, STEP), STEP)
                zb = land3[h, part]
                pref[h, part] = (coef(18, h, g) * zb + coef(19, h, g) * land1[h, part]).astype(BF16)
                land3[h, part] = coef(20, h, g) * zb + coef(21, h, g) * mem[h, part]
            remote(land3.at[h, rows], land3.at[h, rows], s1.at[u], r3.at[u], y, against(g)).start()

    def back_e(u):
        h, g, c, rows = unit(u)
        @pl.when((role(g) == 0) | (role(g) == 3))
        def _():
            remote(mem.at[h, rows], land3.at[h, rows], s0.at[u], r3.at[u], y, along(g)).wait_recv()
            pref[h, rows] = land3[h, rows].astype(BF16)

    def sends_done(g, _):
        part = role(g)
        small = pl.ds(0, STEP)
        h = jnp.right_shift(g, 1)

        def done(sem):
            for c in range(PIECES // 2):
                rows = pl.ds(c * ROWS, ROWS)
                remote(
                    mem.at[h, rows], land1.at[h, rows], sem.at[g * (PIECES // 2) + c], r1.at[0], y, along(g)
                ).wait_send()

        @pl.when((part != 2) | (y < NY - 1))
        def _():
            done(s0)

        @pl.when((part == 1) | (part == 2))
        def _():
            done(s1)

        @pl.when(part == 2)
        def _():
            done(s2)

        @pl.when((part == 2) & (y == NY - 1))
        def _():
            for i in range(NY * NZ // 2):
                @pl.when((g & 1) * (NY * NZ // 2) + i != me)
                def _():
                    remote(
                        mem.at[h, small], fin.at[h], sf.at[g * (NY * NZ // 2) + i], rf.at[h], y, along(g)
                    ).wait_send()
        return 0

    row_id = lax.broadcasted_iota(jnp.int32, (TILE, TILE), 0)
    col_id = lax.broadcasted_iota(jnp.int32, (TILE, TILE), 1)
    lane_id = lax.broadcasted_iota(jnp.int32, (TILE, 128), 1)

    def attend(h, i):
        q = qs[h, i * TILE:(i + 1) * TILE, :]
        bcol = column(cols1, i * TILE, TILE, h, H)
        total = jnp.zeros((TILE, DV), F32)
        den = jnp.zeros((TILE, 1), F32)
        for j in range(i + 1):
            span = slice(j * TILE, (j + 1) * TILE)
            s = lax.dot_general(q, ks[h, span, :], (((1,), (1,)), ((), ())), preferred_element_type=F32)
            p = jnp.exp(arow[pl.ds(h, 1), span] - bcol) * s
            if j == i:
                p = jnp.where(row_id >= col_id, p, 0.0)
            den = den + jnp.sum(p, axis=1, keepdims=True)
            total = total + jnp.dot(p.astype(BF16), vs[h, span, :], preferred_element_type=F32)
        w2 = column(cols2, i * TILE, TILE, h, H)
        acc[h, i * TILE:(i + 1) * TILE, :] = w2 * total
        at = slice(i * TILE, (i + 1) * TILE)
        dens[at, :] = jnp.where(lane_id == h, w2 * den, dens[at, :])

    def finish(h, i):
        at = slice(i * TILE, (i + 1) * TILE)
        q = qs[h, at, :]
        qn = jnp.sum(q.astype(F32) * pnorm[pl.ds(h, 1), :], axis=1, keepdims=True)
        w1 = column(cols2, i * TILE, TILE, h, 0)
        floor = column(cols2, i * TILE, TILE, h, 2 * H)
        den = column(dens, i * TILE, TILE, h, 0)
        inverse = 1.0 / jnp.maximum(jnp.abs(w1 * qn + den), floor)
        carried_term = jnp.dot(q, pref[h], preferred_element_type=F32)
        vs[h, at, :] = ((w1 * carried_term + acc[h, at, :]) * inverse).astype(BF16)

    lag_o = LAG_O + LAG_Y * y
    lag_b = lag_o + LAG_B
    lag_e = lag_b + LAG_E

    def guarded(fn, u):
        @pl.when((u >= 0) & (u < UNITS))
        def _():
            fn(jnp.clip(u, 0, UNITS - 1))

    lag_f = jnp.maximum(jnp.right_shift(lag_e + PIECES - 1, PIECES.bit_length() - 1), max(H - EARLY + 1, LAG_A)) + 1

    def main(hh, _):
        @pl.when(hh + EARLY < H)
        def _():
            summarize(jnp.minimum(hh + EARLY, H - 1), 0)

        @pl.when(hh == H - EARLY)
        def _():
            spread(norms, snorm, rnorm)

        hf = hh - lag_f

        @pl.when(hf == 0)
        def _():
            normals()

        for c in range(PIECES):
            v = hh * PIECES + c
            guarded(first_send, v + LEAD)
            guarded(gather_b, v)
            guarded(own_o, v - lag_o)
            guarded(back_b, v - lag_b)
            guarded(back_e, v - lag_e)

            if c % EACH == 0:
                @pl.when((hh >= LAG_A) & (hh < H + LAG_A))
                def _():
                    h = jnp.clip(hh - LAG_A, 0, H - 1)
                    if c == 0:
                        pltpu.make_async_copy(q_hbm.at[:, 0:DQK], qs.at[h], in_sem.at[2 * H + h]).wait()
                    attend(h, c // EACH)

            if c % EACH == EACH // 2:
                @pl.when((hf >= 0) & (hf < H))
                def _():
                    finish(jnp.clip(hf, 0, H - 1), c // EACH)
        return 0

    max_lag = LAG_O + LAG_Y * (NY - 1) + LAG_B + LAG_E
    lax.fori_loop(0, H + max((max_lag + PIECES - 1) // PIECES, H - EARLY + 1, LAG_A) + 1, main, 0)

    def last(h, _):
        g = 2 * h + jnp.right_shift(me, 3)

        @pl.when((y != NY - 1) | (role(g) != 2))
        def _():
            remote(mem.at[h, pl.ds(0, STEP)], fin.at[h], s0.at[0], rf.at[h], y, along(g)).wait_recv()
        finm_ref[h] = fin[h]
        return 0

    lax.fori_loop(0, H, last, 0)
    lax.fori_loop(0, 2 * H, sends_done, 0)
    spread_done(stats, sstat, rstat)
    spread_done(norms, snorm, rnorm)


def write_out(heads, finm, fins, out_hbm, finm_hbm, norm_ref, stab_ref, sem):
    copies = [
        pltpu.make_async_copy(heads.at[h], out_hbm.at[:, h * DV:(h + 1) * DV], sem.at[h])
        for h in range(H)
    ]
    copies.append(pltpu.make_async_copy(finm, finm_hbm, sem.at[H]))
    for copy in copies:
        copy.start()
    norm_ref[...] = fins[0:H, 0:DQK // (NY * NZ)]
    stab_ref[...] = fins[H:2 * H, 0:1].reshape(H)
    for copy in copies:
        copy.wait()


def shards(query_matrix, key_vectors, value_vectors, input_gate, forget_gate):
    vmem = pl.BlockSpec(memory_space=pltpu.VMEM)
    hbm = pl.BlockSpec(memory_space=pl.ANY)
    dma = pltpu.SemaphoreType.DMA
    ctx = NY * NZ
    heads, final_memory, small = pl.pallas_call(
        kernel,
        out_shape=(
            pltpu.VMEM((H, LEN, DV), BF16),
            pltpu.VMEM((H, DQK // ctx, DV), F32),
            pltpu.VMEM((2 * H, 128), F32),
        ),
        in_specs=[hbm] * 5,
        out_specs=(vmem, vmem, vmem),
        scratch_shapes=[
            pltpu.VMEM((H, LEN, DQK), BF16),
            pltpu.VMEM((H, LEN, DQK), BF16),
            pltpu.VMEM((H, DQK, DV), F32),
            pltpu.VMEM((H, DQK, DV), F32),
            pltpu.VMEM((H, DQK, DV), F32),
            pltpu.VMEM((H, DQK, DV), F32),
            pltpu.VMEM((H, DQK, DV), F32),
            pltpu.VMEM((H, LEN, DV), F32),
            pltpu.VMEM((H, DQK, DV), BF16),
            pltpu.VMEM((H, LEN), F32),
            pltpu.VMEM((H, LEN), F32),
            pltpu.VMEM((LEN, 128), F32),
            pltpu.VMEM((LEN, 128), F32),
            pltpu.VMEM((LEN, 128), F32),
            pltpu.VMEM((128, LEN), F32),
            pltpu.VMEM((H, LEN), F32),
            pltpu.VMEM((2, H, LEN), F32),
            pltpu.VMEM((2, NCOEF, H, DV), F32),
            pltpu.VMEM((ctx, 2 * H, 128), F32),
            pltpu.VMEM((ctx, H, DQK), F32),
            pltpu.VMEM((H, DQK), F32),
            pltpu.VMEM((H, DQK // ctx, DV), F32),
            dma((3 * H,)),
            dma((UNITS,)),
            dma((UNITS,)),
            dma((UNITS,)),
            dma((UNITS,)),
            dma((UNITS,)),
            dma((UNITS,)),
            dma((UNITS * SHARES,)),
            dma((H,)),
            dma((ctx,)),
            dma((ctx,)),
            dma((ctx,)),
            dma((ctx,)),
            dma((2,)),
        ],
        compiler_params=pltpu.CompilerParams(
            collective_id=0, has_side_effects=True, vmem_limit_bytes=57_000_000, fuse_transposed_lhs_in_matmul=True
        ),
        name="mlstm_cell",
    )(query_matrix, key_vectors, value_vectors, input_gate, forget_gate)
    return pl.pallas_call(
        write_out,
        out_shape=(
            jax.ShapeDtypeStruct((LEN, H * DV), BF16),
            jax.ShapeDtypeStruct((H, DQK // ctx, DV), F32),
            jax.ShapeDtypeStruct((H, DQK // ctx), F32),
            jax.ShapeDtypeStruct((H,), F32),
        ),
        in_specs=[hbm, hbm, vmem],
        out_specs=(hbm, hbm, vmem, vmem),
        scratch_shapes=[dma((H + 1,))],
        compiler_params=pltpu.CompilerParams(vmem_limit_bytes=1_000_000),
        name="write_out",
    )(heads, final_memory, small)


def solution(mesh):
    split = Mesh(mesh.devices.reshape(NY, NZ, mesh.shape["seq"]), ("ctx_0", "ctx_1", "seq"))
    return jax.shard_map(
        shards,
        mesh=split,
        in_specs=(
            P(SEQ_CTX, None),
            P(SEQ_CTX, None),
            P(SEQ_CTX, None),
            P(None, SEQ_CTX),
            P(None, SEQ_CTX),
        ),
        out_specs=(P(SEQ_CTX, None), P("seq", CTX, None), P("seq", CTX), P("seq")),
        check_vma=False,
    )
```
